256 devices in a mesh: sp: 64 (over z, y, x_hi), hd: 4 (over x_lo, core).
Axes of the slice: x: 4 (x_hi: 2, x_lo: 2; x = x_hi * 2 + x_lo), y: 4, z: 8, core: 2. Of those that a mesh axis runs over, the one named last changes fastest.
Arguments:
- features: bfloat16 [524288, 256], P(('sp', 'hd')), may hold values from -48 to 48
- point_dest: int32 [524288], P(('sp', 'hd')), may hold values from 0 to 524287, as said below
- cluster: int32 [524288], P(('sp', 'hd')), may hold values from 0 to 131071, as said below
- owner_row: int32 [131072], P(('sp', 'hd')), may hold values from 0 to 131071, as said below
- w_qkv: bfloat16 [3, 256, 256], replicated, may hold values from -1 to 1
- w_out: bfloat16 [256, 256], replicated, may hold values from -0.375 to 0.375
- w_up: bfloat16 [256, 1024], replicated, may hold values from -0.375 to 0.375
- w_down: bfloat16 [1024, 256], replicated, may hold values from -0.1875 to 0.1875
- w_pool: bfloat16 [256, 512], replicated, may hold values from -0.375 to 0.375
Outputs:
- pooled: bfloat16 [131072, 512], P(('sp', 'hd'))
The draws below stay inside these ranges and needn't reach their ends.
Inputs may be any that keep to these rules, and one draw needn't show every extreme that they name: `point_dest`: a permutation; at most 12 of the points of one device (a block of 2048 consecutive entries) go to any one block of 2048 consecutive positions of the new order. `cluster`: on device s (entries s * 2048 to (s + 1) * 2048 - 1) the ids never fall along the points, and each id from s * 512 to (s + 1) * 512 - 1 names one or more of its points. `owner_row`: a permutation; at most 4 of the voxels of one device (a block of 512 consecutive entries) go to any one block of 512 consecutive output rows.
All inputs are finite; a program needn't handle non-finite values.
Results may differ from the reference program's by a relative error of at most 0.0071.
Values may be sent and summed in bfloat16 or wider, within the bound.
A program may use at most 64 MiB of HBM per device.

```python
import jax
import jax.numpy as jnp
from jax import lax

D = 256
H = 16
HS = 16
FF = 1024
D2 = 512
PATCH = 1024
P_DEV = 2048
V_DEV = 512
POINTS = 524288
N_SP = 64
N_HD = 4


def bounded_targets(key, block_count, block_rows, margin):
    base = block_rows // block_count
    subkeys = jax.random.split(key, 6)
    offsets = jax.random.randint(subkeys[0], (block_count // 2,), 0, margin + 1).at[0].set(margin)
    loads = jax.random.permutation(subkeys[1], jnp.concatenate([base + offsets, base - offsets]))
    starts = jnp.cumsum(loads) - loads
    positions = jnp.arange(block_rows, dtype=jnp.int32)
    member = jnp.sum((starts[None, :] <= positions[:, None]).astype(jnp.int32), axis=1) - 1
    first_perm = jax.random.permutation(subkeys[2], block_count)
    second_perm = jax.random.permutation(subkeys[3], block_count)
    slot_perms = jax.vmap(lambda piece: jax.random.permutation(piece, block_rows))(jax.random.split(subkeys[4], block_count))
    row_perms = jax.vmap(lambda piece: jax.random.permutation(piece, block_rows))(jax.random.split(subkeys[5], block_count))
    target_block = second_perm[(first_perm[:, None] + member[None, :]) % block_count]
    target_slot = slot_perms[target_block, positions[None, :]]
    sources = jnp.arange(block_count, dtype=jnp.int32)[:, None] * block_rows + row_perms
    targets = target_block * block_rows + target_slot
    empty = jnp.zeros((block_count * block_rows,), jnp.int32)
    return empty.at[sources.reshape(-1)].set(targets.reshape(-1).astype(jnp.int32))


def draw_point_dest(key, part):
    block_count = N_SP * N_HD
    return bounded_targets(jax.random.fold_in(key, 101), block_count, P_DEV, P_DEV // block_count // 2)


def draw_owner_row(key, part):
    block_count = N_SP * N_HD
    return bounded_targets(jax.random.fold_in(key, 202), block_count, V_DEV, V_DEV // block_count)


def draw_cluster(key, part):
    block_count = N_SP * N_HD
    subkeys = jax.random.split(jax.random.fold_in(key, 303), 2)
    offsets = jax.random.randint(subkeys[0], (block_count, V_DEV // 2), 0, 4).at[:, 0].set(3)
    raw_sizes = jnp.concatenate([4 + offsets, 4 - offsets], axis=1)
    shuffles = jax.vmap(lambda piece: jax.random.permutation(piece, V_DEV))(jax.random.split(subkeys[1], block_count))
    run_sizes = jnp.take_along_axis(raw_sizes, shuffles, axis=1)
    starts = jnp.cumsum(run_sizes, axis=1) - run_sizes
    device_rows = jnp.arange(block_count, dtype=jnp.int32)[:, None]
    markers = jnp.zeros((block_count, P_DEV), jnp.int32).at[device_rows, starts].add(1)
    local_ids = jnp.cumsum(markers, axis=1) - 1
    return (local_ids + device_rows * V_DEV).reshape(-1).astype(jnp.int32)


def draw_features(key, part):
    subkeys = jax.random.split(jax.random.fold_in(key, 404), 1)
    values = jnp.clip(jax.random.normal(subkeys[0], (POINTS, D)), -6.0, 6.0)
    return values.astype(jnp.bfloat16)


def draw_w_qkv(key, part):
    subkeys = jax.random.split(jax.random.fold_in(key, 505), 1)
    values = jnp.clip(jax.random.normal(subkeys[0], (3, D, H * HS)), -4.0, 4.0) * D ** (-0.5)
    return values.astype(jnp.bfloat16)


def normal_values(key, dims, width, reach, held_as=jnp.bfloat16):
    return jnp.clip(width * jax.random.normal(key, dims, jnp.float32), -reach, reach).astype(held_as)


def setup_inputs(seed: int = 0) -> dict:
    keys = jax.random.split(jax.random.key(seed), 10)
    features = draw_features(jax.random.fold_in(keys[9], 71), 0)
    point_dest = draw_point_dest(jax.random.fold_in(keys[9], 71), 0)
    cluster = draw_cluster(jax.random.fold_in(keys[9], 71), 0)
    owner_row = draw_owner_row(jax.random.fold_in(keys[9], 71), 0)
    w_qkv = draw_w_qkv(jax.random.fold_in(keys[9], 71), 0)
    w_out = normal_values(keys[5], (H * HS, D), (H * HS) ** -0.5, 0.375)
    w_up = normal_values(keys[6], (D, FF), D ** -0.5, 0.375)
    w_down = normal_values(keys[7], (FF, D), FF ** -0.5, 0.1875)
    w_pool = normal_values(keys[8], (D, D2), D ** -0.5, 0.375)
    return dict(features=features, point_dest=point_dest, cluster=cluster, owner_row=owner_row, w_qkv=w_qkv, w_out=w_out, w_up=w_up, w_down=w_down, w_pool=w_pool)


EPSILON = 1e-05

def normalize(values):
    center = lax.optimization_barrier(jnp.mean(values, axis=-1, keepdims=True))
    shifted = values - center
    spread = lax.optimization_barrier(jnp.mean(shifted * shifted, axis=-1, keepdims=True))
    return shifted * lax.rsqrt(spread + EPSILON)

def bfloat_round(values):
    return lax.optimization_barrier(values.astype(jnp.bfloat16)).astype(jnp.float32)

def reference(features, point_dest, cluster, owner_row, w_qkv, w_out, w_up, w_down, w_pool):
    total_points = features.shape[0]
    points = jnp.zeros_like(features).at[point_dest].set(features)

    def patch_layer(number):
        inputs = lax.dynamic_slice_in_dim(points, number * PATCH, PATCH, 0).astype(jnp.float32)
        normed = normalize(inputs).astype(jnp.bfloat16)
        queries = jnp.dot(normed, w_qkv[0], preferred_element_type=jnp.float32).astype(jnp.bfloat16)
        key_rows = jnp.dot(normed, w_qkv[1], preferred_element_type=jnp.float32).astype(jnp.bfloat16)
        value_rows = jnp.dot(normed, w_qkv[2], preferred_element_type=jnp.float32).astype(jnp.bfloat16)
        query_heads = queries.astype(jnp.float32).reshape(PATCH, H, HS)
        key_heads = key_rows.astype(jnp.float32).reshape(PATCH, H, HS)
        value_heads = value_rows.astype(jnp.float32).reshape(PATCH, H, HS)
        scores = jnp.einsum('qhd,khd->hqk', query_heads, key_heads) * HS ** (-0.5)
        weights = bfloat_round(jax.nn.softmax(scores, axis=-1))
        attended = jnp.einsum('hqk,khd->qhd', weights, value_heads).reshape(PATCH, H * HS).astype(jnp.bfloat16)
        attn_total = jnp.dot(attended, w_out, preferred_element_type=jnp.float32)
        middle = inputs + attn_total
        normed_two = normalize(middle).astype(jnp.bfloat16)
        hidden = jax.nn.gelu(jnp.dot(normed_two, w_up, preferred_element_type=jnp.float32), approximate=False).astype(jnp.bfloat16)
        mlp_total = jnp.dot(hidden, w_down, preferred_element_type=jnp.float32)
        return (middle + mlp_total).astype(jnp.bfloat16)
    finals = lax.map(patch_layer, jnp.arange(total_points // PATCH, dtype=jnp.int32)).reshape(total_points, D)
    voxel_total = owner_row.shape[0]
    totals = jax.ops.segment_sum(finals.astype(jnp.float32), cluster, num_segments=voxel_total)
    tallies = jax.ops.segment_sum(jnp.ones((total_points,), jnp.float32), cluster, num_segments=voxel_total)
    means = (totals / tallies[:, None]).astype(jnp.bfloat16)
    projected = jnp.dot(means, w_pool, preferred_element_type=jnp.float32)
    activated = jax.nn.gelu(normalize(projected), approximate=False).astype(jnp.bfloat16)
    return jnp.zeros((voxel_total, D2), jnp.bfloat16).at[owner_row].set(activated)
```

```python
import functools
import jax
import jax.numpy as jnp
from jax import lax
from jax.experimental import pallas as pl
from jax.experimental.pallas import tpu as pltpu
from jax.sharding import PartitionSpec as P

BF = jnp.bfloat16
F32 = jnp.float32
I32 = jnp.int32
HS = 16
PATCH = 1024
EPSILON = 1e-05
LOG2E = 1.4426950408889634
SCALE = HS ** (-0.5) * LOG2E
SAFE = 100.0


def normalize(values):
    center = jnp.mean(values, axis=-1, keepdims=True)
    shifted = values - center
    spread = jnp.mean(shifted * shifted, axis=-1, keepdims=True)
    return shifted * lax.rsqrt(spread + EPSILON)


def gelu(values):
    return 0.5 * values * (1.0 + lax.erf(values * (0.5**0.5)))


def mm(a, b):
    return jnp.dot(a, b, preferred_element_type=F32)


def layer_kernel(
    points_ref, ids_ref, wqkv_ref, wout_ref, wup_ref, wdown_ref, means_ref,
    wq_s, wv_s, k_s, q_s, v_s, att_s, fin_s,
):
    rows_all, width = points_ref.shape
    heads = width // HS
    blk = 256
    groups = width // 128
    wq_s[...] = wqkv_ref[0].T
    wv_s[...] = wqkv_ref[2].T
    v_s[:, HS:, :] = jnp.ones((heads, HS, PATCH), BF)
    head_mask = (
        lax.broadcasted_iota(I32, (width, 128), 0) // HS
        == lax.broadcasted_iota(I32, (width, 128), 1)
    ).astype(BF)

    def patch(number, carry):
        base = number * PATCH

        def project(i, bound):
            qmax, kmax = bound
            r0 = pl.multiple_of(i * blk, blk)
            x = points_ref[pl.ds(pl.multiple_of(base + r0, blk), blk), :].astype(F32)
            normed = normalize(x).astype(BF)
            keys = mm(normed, wqkv_ref[1])
            for g in range(groups):
                k_s[g, pl.ds(r0, blk), :] = keys[:, g * 128 : (g + 1) * 128].astype(BF)
            nt = (((1,), (1,)), ((), ()))
            queries = lax.dot_general(wq_s[...], normed, nt, preferred_element_type=F32)
            values = lax.dot_general(wv_s[...], normed, nt, preferred_element_type=F32)
            q_s[:, pl.ds(r0, blk)] = queries.astype(BF)
            v_s[:, 0:HS, pl.ds(r0, blk)] = values.astype(BF).reshape(heads, HS, blk)
            knorm = mm((keys * keys).astype(BF), head_mask)
            qnorm = jnp.sum((queries * queries).reshape(heads, HS, blk), axis=1)
            return (jnp.maximum(qmax, qnorm), jnp.maximum(kmax, jnp.max(knorm, axis=0, keepdims=True)))

        qmax, kmax = lax.fori_loop(
            0, PATCH // blk, project,
            (jnp.zeros((heads, blk), F32), jnp.zeros((1, 128), F32)),
        )
        bound = 1.05 * SCALE * SCALE * jnp.max(qmax) * jnp.max(kmax)
        qb = 512
        sub = lax.broadcasted_iota(I32, (128, qb), 0) // HS

        def attend(shifted):
            def head(h, c):
                g = h // 8
                r0 = pl.multiple_of(h * HS, HS)
                for q0 in range(0, PATCH, qb):
                    q = q_s[pl.ds(r0, HS), q0 : q0 + qb]
                    q = jnp.concatenate([q] * 8, axis=0)
                    q = jnp.where(sub == h % 8, q, jnp.zeros_like(q))
                    scores = mm(k_s[g], q)
                    if shifted:
                        scores = scores - jnp.max(scores, axis=0, keepdims=True)
                    raised = jnp.exp2(scores * SCALE).astype(BF)
                    out = mm(v_s[h], raised)
                    att_s[pl.ds(r0, HS), q0 : q0 + qb] = (out[:HS] / out[HS : HS + 1]).astype(BF)
                return c

            lax.fori_loop(0, heads, head, 0)

        @pl.when(bound <= SAFE * SAFE)
        def _():
            attend(False)

        @pl.when(jnp.logical_not(bound <= SAFE * SAFE))
        def _():
            attend(True)

        def mlp(i, c):
            r0 = pl.multiple_of(i * blk, blk)
            rows = pl.ds(pl.multiple_of(base + r0, blk), blk)
            attended = att_s[:, pl.ds(r0, blk)].T
            middle = points_ref[rows, :].astype(F32) + mm(attended, wout_ref[...])
            normed = normalize(middle).astype(BF)
            total = middle
            hidden = gelu(mm(normed, wup_ref[...])).astype(BF)
            total = total + mm(hidden, wdown_ref[...])
            fin_s[rows, :] = total.astype(BF)
            return c

        lax.fori_loop(0, PATCH // blk, mlp, 0)
        return carry

    lax.fori_loop(0, rows_all // PATCH, patch, 0)

    voxels = means_ref.shape[0]
    vb = 128

    def pool(i, c):
        v0 = pl.multiple_of(i * vb, vb)
        marks = (
            lax.broadcasted_iota(I32, (vb, rows_all), 0) + v0 == ids_ref[...]
        )
        marks = jnp.where(marks, 1.0, 0.0).astype(F32)
        tally = jnp.sum(marks, axis=1, keepdims=True)
        totals = mm(marks.astype(BF), fin_s[...])
        means_ref[pl.ds(v0, vb), :] = (totals / tally).astype(BF)
        return c

    lax.fori_loop(0, voxels // vb, pool, 0)


def layer(points, ids, w_qkv, w_out, w_up, w_down, voxels):
    rows, width = points.shape
    heads = width // HS
    vm = pl.BlockSpec(memory_space=pltpu.VMEM)
    return pl.pallas_call(
        layer_kernel,
        out_shape=jax.ShapeDtypeStruct((voxels, width), BF),
        in_specs=[vm] * 6,
        out_specs=vm,
        scratch_shapes=[
            pltpu.VMEM((width, width), BF),
            pltpu.VMEM((width, width), BF),
            pltpu.VMEM((width // 128, PATCH, 128), BF),
            pltpu.VMEM((width, PATCH), BF),
            pltpu.VMEM((heads, 2 * HS, PATCH), BF),
            pltpu.VMEM((width, PATCH), BF),
            pltpu.VMEM((rows, width), BF),
        ],
        compiler_params=pltpu.CompilerParams(vmem_limit_bytes=56 * 2**20),
        name="layer",
    )(points, ids, w_qkv, w_out, w_up, w_down)


def pack_rows(row_data, target, block_len, peer_count, capacity):
    owner_block = target // block_len
    slot_number = target % block_len
    onehot = (owner_block[:, None] == jnp.arange(peer_count, dtype=jnp.int32)[None, :]).astype(
        jnp.int32
    )
    before = jnp.cumsum(onehot, axis=0) - onehot
    positions = owner_block * capacity + jnp.sum(before * onehot, axis=1)
    packed = (
        jnp.zeros((peer_count * capacity, row_data.shape[1]), row_data.dtype)
        .at[positions]
        .set(row_data)
    )
    slot_ids = (
        jnp.full((peer_count * capacity,), block_len, jnp.int32).at[positions].set(slot_number)
    )
    return (packed, slot_ids)


def place_rows(arrived, slot_ids, block_len):
    return (
        jnp.zeros((block_len, arrived.shape[1]), arrived.dtype)
        .at[slot_ids]
        .set(arrived, mode="drop")
    )


def pack_voxels(row_data, owner_row, voxel_local, outer_count, inner_count):
    device_count = outer_count * inner_count
    capacity = 2 * (voxel_local // device_count)
    width = row_data.shape[1]
    packed, slot_ids = pack_rows(row_data, owner_row, voxel_local, device_count, capacity)
    return (
        packed.reshape(outer_count, inner_count, capacity, width),
        slot_ids.reshape(outer_count, inner_count, capacity),
    )


def per_device(features, point_dest, cluster, owner_row, w_qkv, w_out, w_up, w_down, w_pool):
    local_points = features.shape[0]
    model_width = features.shape[1]
    voxel_local = owner_row.shape[0]
    outer_count = lax.axis_size("sp")
    inner_count = lax.axis_size("hd")
    device_count = outer_count * inner_count
    device_number = lax.axis_index("sp") * inner_count + lax.axis_index("hd")
    base_rows = local_points // device_count
    capacity = base_rows + base_rows // 2
    packed, slot_ids = pack_rows(features, point_dest, local_points, device_count, capacity)
    packed = packed.reshape(outer_count, inner_count, capacity, model_width)
    slot_ids = slot_ids.reshape(outer_count, inner_count, capacity)
    arrived, arrived_slots = (
        lax.all_to_all(
            lax.all_to_all(packed, "sp", split_axis=0, concat_axis=0, tiled=True),
            "hd",
            split_axis=1,
            concat_axis=1,
            tiled=True,
        ),
        lax.all_to_all(
            lax.all_to_all(slot_ids, "sp", split_axis=0, concat_axis=0, tiled=True),
            "hd",
            split_axis=1,
            concat_axis=1,
            tiled=True,
        ),
    )
    points = place_rows(arrived.reshape(-1, model_width), arrived_slots.reshape(-1), local_points)
    local_ids = cluster - device_number * voxel_local
    means = layer(
        points, local_ids.reshape(1, local_points), w_qkv, w_out, w_up, w_down, voxel_local
    )
    sent_rows, sent_slots = pack_voxels(means, owner_row, voxel_local, outer_count, inner_count)
    got_rows, got_slots = (
        lax.all_to_all(
            lax.all_to_all(sent_rows, "sp", split_axis=0, concat_axis=0, tiled=True),
            "hd",
            split_axis=1,
            concat_axis=1,
            tiled=True,
        ),
        lax.all_to_all(
            lax.all_to_all(sent_slots, "sp", split_axis=0, concat_axis=0, tiled=True),
            "hd",
            split_axis=1,
            concat_axis=1,
            tiled=True,
        ),
    )
    placed = place_rows(
        got_rows.reshape(-1, means.shape[1]), got_slots.reshape(-1), voxel_local
    )
    projected = mm(placed, w_pool)
    return gelu(normalize(projected)).astype(BF)


def solution(mesh):
    return jax.shard_map(
        per_device,
        mesh=mesh,
        in_specs=(
            P(("sp", "hd"), None),
            P(("sp", "hd")),
            P(("sp", "hd")),
            P(("sp", "hd")),
            P(),
            P(),
            P(),
            P(),
            P(),
        ),
        out_specs=P(("sp", "hd"), None),
        check_vma=False,
    )
```

```python
import functools
import jax
import jax.numpy as jnp
from jax import lax
from jax.experimental import pallas as pl
from jax.experimental.pallas import tpu as pltpu
from jax.sharding import PartitionSpec as P

BF = jnp.bfloat16
F32 = jnp.float32
I32 = jnp.int32
HS = 16
PATCH = 1024
EPSILON = 1e-05
LOG2E = 1.4426950408889634
SCALE = HS ** (-0.5) * LOG2E
SAFE = 100.0


def normalize(values):
    center = jnp.mean(values, axis=-1, keepdims=True)
    shifted = values - center
    spread = jnp.mean(shifted * shifted, axis=-1, keepdims=True)
    return shifted * lax.rsqrt(spread + EPSILON)


def gelu(values):
    return 0.5 * values * (1.0 + lax.erf(values * (0.5**0.5)))


def mm(a, b):
    return jnp.dot(a, b, preferred_element_type=F32)


def layer_kernel(
    points_ref, ids_ref, wqkv_ref, wout_ref, wup_ref, wdown_ref, means_ref,
    wq_s, wv_s, k_s, q_s, v_s, att_s, fin_s,
):
    rows_all, width = points_ref.shape
    heads = width // HS
    blk = 256
    groups = width // 128
    wq_s[...] = wqkv_ref[0].T
    wv_s[...] = wqkv_ref[2].T
    v_s[:, HS:, :] = jnp.ones((heads, HS, PATCH), BF)
    head_mask = (
        lax.broadcasted_iota(I32, (width, 128), 0) // HS
        == lax.broadcasted_iota(I32, (width, 128), 1)
    ).astype(BF)

    def patch(number, carry):
        base = number * PATCH

        def project(i, bound):
            qmax, kmax = bound
            r0 = pl.multiple_of(i * blk, blk)
            x = points_ref[pl.ds(pl.multiple_of(base + r0, blk), blk), :].astype(F32)
            normed = normalize(x).astype(BF)
            keys = mm(normed, wqkv_ref[1])
            for g in range(groups):
                k_s[g, pl.ds(r0, blk), :] = keys[:, g * 128 : (g + 1) * 128].astype(BF)
            nt = (((1,), (1,)), ((), ()))
            queries = lax.dot_general(wq_s[...], normed, nt, preferred_element_type=F32)
            values = lax.dot_general(wv_s[...], normed, nt, preferred_element_type=F32)
            q_s[:, pl.ds(r0, blk)] = queries.astype(BF)
            v_s[:, 0:HS, pl.ds(r0, blk)] = values.astype(BF).reshape(heads, HS, blk)
            knorm = mm((keys * keys).astype(BF), head_mask)
            qnorm = jnp.sum((queries * queries).reshape(heads, HS, blk), axis=1)
            return (jnp.maximum(qmax, qnorm), jnp.maximum(kmax, jnp.max(knorm, axis=0, keepdims=True)))

        qmax, kmax = lax.fori_loop(
            0, PATCH // blk, project,
            (jnp.zeros((heads, blk), F32), jnp.zeros((1, 128), F32)),
        )
        bound = 1.05 * SCALE * SCALE * jnp.max(qmax) * jnp.max(kmax)
        qb = 512
        sub = lax.broadcasted_iota(I32, (128, qb), 0) // HS

        def attend(shifted):
            def head(h, c):
                g = h // 8
                r0 = pl.multiple_of(h * HS, HS)
                for q0 in range(0, PATCH, qb):
                    q = q_s[pl.ds(r0, HS), q0 : q0 + qb]
                    q = jnp.concatenate([q] * 8, axis=0)
                    q = jnp.where(sub == h % 8, q, jnp.zeros_like(q))
                    scores = mm(k_s[g], q)
                    if shifted:
                        scores = scores - jnp.max(scores, axis=0, keepdims=True)
                    raised = jnp.exp2(scores * SCALE).astype(BF)
                    out = mm(v_s[h], raised)
                    att_s[pl.ds(r0, HS), q0 : q0 + qb] = (out[:HS] / out[HS : HS + 1]).astype(BF)
                return c

            lax.fori_loop(0, heads, head, 0)

        @pl.when(bound <= SAFE * SAFE)
        def _():
            attend(False)

        @pl.when(jnp.logical_not(bound <= SAFE * SAFE))
        def _():
            attend(True)

        def mlp(i, c):
            r0 = pl.multiple_of(i * blk, blk)
            rows = pl.ds(pl.multiple_of(base + r0, blk), blk)
            attended = att_s[:, pl.ds(r0, blk)].T
            middle = points_ref[rows, :].astype(F32) + mm(attended, wout_ref[...])
            normed = normalize(middle).astype(BF)
            total = middle
            hidden = gelu(mm(normed, wup_ref[...])).astype(BF)
            total = total + mm(hidden, wdown_ref[...])
            fin_s[rows, :] = total.astype(BF)
            return c

        lax.fori_loop(0, PATCH // blk, mlp, 0)
        return carry

    lax.fori_loop(0, rows_all // PATCH, patch, 0)

    voxels = means_ref.shape[0]
    vb = 128

    def pool(i, c):
        v0 = pl.multiple_of(i * vb, vb)
        marks = (
            lax.broadcasted_iota(I32, (vb, rows_all), 0) + v0 == ids_ref[...]
        )
        marks = jnp.where(marks, 1.0, 0.0).astype(F32)
        tally = jnp.sum(marks, axis=1, keepdims=True)
        totals = mm(marks.astype(BF), fin_s[...])
        means_ref[pl.ds(v0, vb), :] = (totals / tally).astype(BF)
        return c

    lax.fori_loop(0, voxels // vb, pool, 0)


def layer(points, ids, w_qkv, w_out, w_up, w_down, voxels):
    rows, width = points.shape
    heads = width // HS
    vm = pl.BlockSpec(memory_space=pltpu.VMEM)
    return pl.pallas_call(
        layer_kernel,
        out_shape=jax.ShapeDtypeStruct((voxels, width), BF),
        in_specs=[vm] * 6,
        out_specs=vm,
        scratch_shapes=[
            pltpu.VMEM((width, width), BF),
            pltpu.VMEM((width, width), BF),
            pltpu.VMEM((width // 128, PATCH, 128), BF),
            pltpu.VMEM((width, PATCH), BF),
            pltpu.VMEM((heads, 2 * HS, PATCH), BF),
            pltpu.VMEM((width, PATCH), BF),
            pltpu.VMEM((rows, width), BF),
        ],
        compiler_params=pltpu.CompilerParams(vmem_limit_bytes=56 * 2**20),
        name="layer",
    )(points, ids, w_qkv, w_out, w_up, w_down)


PLANES = 8
SIDE = 32
DEVS = PLANES * SIDE
MESH = pl.DeviceIdType.MESH


def turn(q):
    sign = 1 - 2 * (q % 2)
    return (PLANES + sign * (PLANES // 2 - q // 2)) % PLANES * ((q + PLANES - 1) // PLANES)


class Links:
    def __init__(self, inner):
        self.inner = inner
        me = lax.axis_index("sp") * inner + lax.axis_index("hd")
        self.plane = me // SIDE
        self.spot = me % SIDE

    def at(self, plane, spot):
        device = plane * SIDE + spot
        return (device // self.inner, device % self.inner)

    def above(self, k):
        return self.at((self.plane + k) % PLANES, self.spot)

    def beside(self, j):
        return self.at(self.plane, (self.spot + j) % SIDE)

    def greet(self):
        barrier = pltpu.get_barrier_semaphore()

        def up(k, c):
            pl.semaphore_signal(barrier, inc=1, device_id=self.above(k), device_id_type=MESH)
            return c

        def side(j, c):
            pl.semaphore_signal(barrier, inc=1, device_id=self.beside(j), device_id_type=MESH)
            return c

        lax.fori_loop(1, PLANES, up, 0)
        lax.fori_loop(1, SIDE, side, 0)

    def meet(self, ready):
        pl.semaphore_wait(pltpu.get_barrier_semaphore(), PLANES - 1 + SIDE - 1)

        def up(k, c):
            pl.semaphore_signal(ready, inc=1, device_id=self.above(k), device_id_type=MESH)
            return c

        lax.fori_loop(1, PLANES, up, 0)

    def send_all(self, streams, ready):
        def one(k, j):
            to = ((self.plane + k) % PLANES, (self.spot + j) % SIDE)
            device = self.at(*to)
            for source, target, sent, got in streams:
                pltpu.make_async_remote_copy(
                    source.at[to], target.at[self.plane, self.spot], sent.at[k], got.at[k],
                    device_id=device, device_id_type=MESH,
                ).start()

        def near(j, c):
            one(0, j)
            return c

        lax.fori_loop(1, SIDE, near, 0)
        pl.semaphore_wait(ready, PLANES - 1)

        def far(n, c):
            one(turn(1 + n // SIDE), n % SIDE)
            return c

        lax.fori_loop(0, (PLANES - 1) * SIDE, far, 0)
        for source, target, _, _ in streams:
            target[self.plane, self.spot] = source[self.plane, self.spot]

    def arrived(self, streams, k, count):
        source = (self.plane + PLANES - k) % PLANES
        for _, target, sent, got in streams:
            held = target.at[source, pl.ds(0, count)]
            pltpu.make_async_copy(held, held, sent.at[k]).wait()
            pltpu.make_async_copy(held, held, got.at[k]).wait()
        return source


def rank_rows(target_ref, key_ref, block, full):
    step = 256
    sub = lax.broadcasted_iota(I32, (DEVS, step), 0)
    lane = lax.broadcasted_iota(I32, (DEVS, step), 1)
    before = jnp.where(sub < lane, 1.0, 0.0).astype(BF)
    rep = lax.broadcasted_iota(I32, (128, step), 0) % 8
    nt = (((1,), (1,)), ((), ()))

    def ranks(b, carry):
        seen, *sums = carry
        r0 = pl.multiple_of(b * step, step)
        target = target_ref[:, pl.ds(r0, step)]
        owner = target // block
        tag = target - owner * block + 1
        mark = jnp.where(sub == owner, 1.0, 0.0)
        marks = mark.astype(BF)
        prior = mm(marks, before) + seen
        rank = jnp.sum(mark * prior, axis=0, keepdims=True).astype(I32)
        key_ref[:, pl.ds(r0, step)] = owner * 16 + rank
        high = (tag // 16).astype(F32)
        low = (tag % 16).astype(F32)

        def gather(values, position):
            picked = jnp.where(rank == position, values, 0.0).astype(BF)
            return lax.dot_general(marks, picked, nt, preferred_element_type=F32)

        found = [gather(high, full + rep % 4), gather(low, full + rep % 4)]
        if full:
            found += [gather(high, rep), gather(low, rep)]
        sums = [s + f for s, f in zip(sums, found)]
        return (seen + jnp.sum(mark, axis=1, keepdims=True), *sums)

    zero = jnp.zeros((DEVS, 128), F32)
    count = target_ref.shape[1]
    _, *sums = lax.fori_loop(
        0, count // step, ranks, (jnp.zeros((DEVS, 1), F32),) + (zero,) * (4 if full else 2)
    )
    tags = [(sums[i] * 16.0 + sums[i + 1]).astype(I32) for i in range(0, len(sums), 2)]
    return tags


def pack_rows(x_ref, key_ref, send_ref, full):
    count, width = x_ref.shape
    half = width // 2
    tiles = send_ref.shape[2]
    spots = lax.broadcasted_iota(I32, (256, count), 0)
    first = lax.broadcasted_iota(I32, (SIDE, 8, half), 1) < 4

    def pack(z, c):
        base = z * SIDE

        def rows_of(rank):
            wanted = (base + spots // 8) * 16 + rank
            picks = jnp.where(key_ref[...] == wanted, 1.0, 0.0).astype(BF)
            rows = mm(picks, x_ref[...])
            return rows[:, :half].reshape(SIDE, 8, half), rows[:, half:].reshape(SIDE, 8, half)

        if full:
            left, right = rows_of(spots % 8)
            send_ref[z, :, 0] = left.astype(BF)
            send_ref[z, :, 1] = right.astype(BF)
        left, right = rows_of(full + spots % 4)
        send_ref[z, :, tiles - 1] = jnp.where(first, left, right).astype(BF)
        return c

    lax.fori_loop(0, PLANES, pack, 0)


def place_rows(got_ref, source, marks, out_ref, full):
    block, width = out_ref.shape
    half = width // 2
    tiles = got_ref.shape[2]
    chunk = min(block, 512)
    first = lax.broadcasted_iota(I32, (SIDE, 8, half), 1) < 4
    weights = []
    if full:
        left = got_ref[source, :, 0].astype(F32).reshape(256, half)
        right = got_ref[source, :, 1].astype(F32).reshape(256, half)
        weights.append(jnp.concatenate([left, right], axis=1).astype(BF))
    mixed = got_ref[source, :, tiles - 1].astype(F32)
    left = jnp.where(first, mixed, 0.0).reshape(256, half)
    right = jnp.where(first, 0.0, mixed).reshape(256, half)
    weights.append(jnp.concatenate([left, right], axis=1).astype(BF))
    weights = jnp.concatenate(weights, axis=0)
    rows = lax.broadcasted_iota(I32, (chunk, marks.shape[1]), 0) + 1

    def some(i, c):
        r0 = pl.multiple_of(i * chunk, chunk)
        picks = jnp.where(marks == rows + r0, 1.0, 0.0).astype(BF)
        at_rows = pl.ds(r0, chunk)
        out_ref[at_rows, :] = (out_ref[at_rows, :].astype(F32) + mm(picks, weights)).astype(BF)
        return c

    lax.fori_loop(0, block // chunk, some, 0)


def spread_kernel(
    full, inner, voxels, x_ref, target_ref, owner_ref, out_ref, key_out, marks_out,
    key_s, send_s, tags_s, got_s, seen_s, d_send, d_recv, t_send, t_recv, ready,
):
    links = Links(inner)
    links.greet()
    block = out_ref.shape[0]
    second, first = rank_rows(target_ref, key_s, block, full)
    (third,) = rank_rows(owner_ref, key_out, voxels, 0)
    lane = lax.broadcasted_iota(I32, (DEVS, 128), 1) // 8
    spot = links.spot % 16
    tags = jnp.where(lane == spot, first + 4096 * second, 0)
    tags = jnp.where(lane == (spot + 8) % 16, third, tags)
    tags_s[...] = tags.reshape(PLANES, SIDE, 1, 128)
    pack_rows(x_ref, key_s, send_s, full)
    out_ref[...] = jnp.zeros_like(out_ref)
    links.meet(ready)
    streams = ((tags_s, seen_s, t_send, t_recv), (send_s, got_s, d_send, d_recv))
    links.send_all(streams, ready)
    low = lax.broadcasted_iota(I32, (1, 128), 1) < 64

    def land(k, count):
        source = links.arrived(streams, k, count)
        points, later = [], []
        for part in range(2):
            a = jnp.sum(seen_s[source, part * 16 : part * 16 + 8], axis=0)
            b = jnp.sum(seen_s[source, part * 16 + 8 : part * 16 + 16], axis=0)
            points.append(jnp.where(low, a, b))
            other = jnp.where(low, b, a)
            later.append(jnp.concatenate([other[:, 64:], other[:, :64]], axis=1))
        points = jnp.concatenate(points, axis=1)
        marks_out[source] = jnp.concatenate(later, axis=1)
        marks = jnp.concatenate([points % 4096, points // 4096], axis=1)
        place_rows(got_s, source, marks, out_ref, full)

    land(0, SIDE - 1)

    def more(q, c):
        land(turn(q), SIDE)
        return c

    lax.fori_loop(1, PLANES, more, 0)


def spread(x, target, owner, capacity, inner):
    count, width = x.shape
    voxels = owner.shape[1]
    vm = pl.BlockSpec(memory_space=pltpu.VMEM)
    data = pltpu.VMEM((PLANES, SIDE, capacity // 4, 8, width // 2), BF)
    tags = pltpu.VMEM((PLANES, SIDE, 1, 128), I32)
    return pl.pallas_call(
        functools.partial(spread_kernel, capacity - 4, inner, voxels),
        out_shape=(
            jax.ShapeDtypeStruct((count, width), BF),
            jax.ShapeDtypeStruct((1, voxels), I32),
            jax.ShapeDtypeStruct((PLANES, 1, 256), I32),
        ),
        in_specs=[vm] * 3,
        out_specs=[vm] * 3,
        scratch_shapes=[pltpu.VMEM((1, count), I32), data, tags, data, tags]
        + [pltpu.SemaphoreType.DMA((PLANES,))] * 4
        + [pltpu.SemaphoreType.REGULAR],
        compiler_params=pltpu.CompilerParams(
            collective_id=1, has_side_effects=True, vmem_limit_bytes=56 * 2**20
        ),
        name="spread",
    )(x, target, owner)


def gather_kernel(
    inner, x_ref, key_ref, marks_ref, out_ref, send_s, got_s, d_send, d_recv, ready
):
    links = Links(inner)
    links.greet()
    pack_rows(x_ref, key_ref, send_s, 0)
    out_ref[...] = jnp.zeros_like(out_ref)
    links.meet(ready)
    streams = ((send_s, got_s, d_send, d_recv),)
    links.send_all(streams, ready)

    def land(k, count):
        source = links.arrived(streams, k, count)
        place_rows(got_s, source, marks_ref[source], out_ref, 0)

    land(0, SIDE - 1)

    def more(q, c):
        land(turn(q), SIDE)
        return c

    lax.fori_loop(1, PLANES, more, 0)


def gather(x, key, marks, inner):
    count, width = x.shape
    vm = pl.BlockSpec(memory_space=pltpu.VMEM)
    data = pltpu.VMEM((PLANES, SIDE, 1, 8, width // 2), BF)
    return pl.pallas_call(
        functools.partial(gather_kernel, inner),
        out_shape=jax.ShapeDtypeStruct((count, width), BF),
        in_specs=[vm] * 3,
        out_specs=vm,
        scratch_shapes=[data, data]
        + [pltpu.SemaphoreType.DMA((PLANES,))] * 2
        + [pltpu.SemaphoreType.REGULAR],
        compiler_params=pltpu.CompilerParams(
            collective_id=2, has_side_effects=True, vmem_limit_bytes=56 * 2**20
        ),
        name="gather",
    )(x, key, marks)


def finish_kernel(x_ref, w_ref, out_ref):
    block = 128

    def some(i, c):
        rows = pl.ds(pl.multiple_of(i * block, block), block)
        out_ref[rows, :] = gelu(normalize(mm(x_ref[rows, :], w_ref[...]))).astype(BF)
        return c

    lax.fori_loop(0, x_ref.shape[0] // block, some, 0)


def finish(x, w):
    vm = pl.BlockSpec(memory_space=pltpu.VMEM)
    return pl.pallas_call(
        finish_kernel,
        out_shape=jax.ShapeDtypeStruct((x.shape[0], w.shape[1]), BF),
        in_specs=[vm] * 2,
        out_specs=vm,
        name="finish",
    )(x, w)


def per_device(features, point_dest, cluster, owner_row, w_qkv, w_out, w_up, w_down, w_pool):
    inner = lax.axis_size("hd")
    voxels = owner_row.shape[0]
    me = lax.axis_index("sp") * inner + lax.axis_index("hd")
    points, key, marks = spread(
        features, point_dest.reshape(1, -1), owner_row.reshape(1, -1), 12, inner
    )
    local_ids = (cluster - me * voxels).reshape(1, -1)
    means = layer(points, local_ids, w_qkv, w_out, w_up, w_down, voxels)
    return finish(gather(means, key, marks, inner), w_pool)


def solution(mesh):
    rows = P(("sp", "hd"), None)
    line = P(("sp", "hd"))
    return jax.shard_map(
        per_device,
        mesh=mesh,
        in_specs=(rows, line, line, line, P(), P(), P(), P(), P()),
        out_specs=rows,
        check_vma=False,
    )
```

```python
import functools
import jax
import jax.numpy as jnp
from jax import lax
from jax.experimental import pallas as pl
from jax.experimental.pallas import tpu as pltpu
from jax.sharding import PartitionSpec as P

BF = jnp.bfloat16
F32 = jnp.float32
I32 = jnp.int32
HS = 16
PATCH = 1024
EPSILON = 1e-05
LOG2E = 1.4426950408889634
SCALE = HS ** (-0.5) * LOG2E
SAFE = 100.0


def normalize(values):
    center = jnp.mean(values, axis=-1, keepdims=True)
    shifted = values - center
    spread = jnp.mean(shifted * shifted, axis=-1, keepdims=True)
    return shifted * lax.rsqrt(spread + EPSILON)


def gelu(values):
    return 0.5 * values * (1.0 + lax.erf(values * (0.5**0.5)))


def mm(a, b):
    return jnp.dot(a, b, preferred_element_type=F32)


def attention_kernel(
    points_ref, wqkv_ref, att_ref, wq_s, wv_s, k_s, q_s, v_s,
):
    rows_all, width = points_ref.shape
    heads = width // HS
    blk = 256
    groups = width // 128
    wq_s[...] = wqkv_ref[0].T
    wv_s[...] = wqkv_ref[2].T
    v_s[:, HS:, :] = jnp.ones((heads, HS, PATCH), BF)
    head_mask = (
        lax.broadcasted_iota(I32, (width, 128), 0) // HS
        == lax.broadcasted_iota(I32, (width, 128), 1)
    ).astype(BF)

    def patch(number, carry):
        base = number * PATCH

        def project(i, bound):
            qmax, kmax = bound
            r0 = pl.multiple_of(i * blk, blk)
            x = points_ref[pl.ds(pl.multiple_of(base + r0, blk), blk), :].astype(F32)
            normed = normalize(x).astype(BF)
            keys = mm(normed, wqkv_ref[1])
            for g in range(groups):
                k_s[g, pl.ds(r0, blk), :] = keys[:, g * 128 : (g + 1) * 128].astype(BF)
            nt = (((1,), (1,)), ((), ()))
            queries = lax.dot_general(wq_s[...], normed, nt, preferred_element_type=F32)
            values = lax.dot_general(wv_s[...], normed, nt, preferred_element_type=F32)
            q_s[:, pl.ds(r0, blk)] = queries.astype(BF)
            v_s[:, 0:HS, pl.ds(r0, blk)] = values.astype(BF).reshape(heads, HS, blk)
            knorm = mm((keys * keys).astype(BF), head_mask)
            qnorm = jnp.sum((queries * queries).reshape(heads, HS, blk), axis=1)
            return (jnp.maximum(qmax, qnorm), jnp.maximum(kmax, jnp.max(knorm, axis=0, keepdims=True)))

        qmax, kmax = lax.fori_loop(
            0, PATCH // blk, project,
            (jnp.zeros((heads, blk), F32), jnp.zeros((1, 128), F32)),
        )
        bound = 1.05 * SCALE * SCALE * jnp.max(qmax) * jnp.max(kmax)
        qb = 512
        sub = lax.broadcasted_iota(I32, (128, qb), 0) // HS

        def attend(shifted):
            def head(h, c):
                g = h // 8
                r0 = pl.multiple_of(h * HS, HS)
                for q0 in range(0, PATCH, qb):
                    q = q_s[pl.ds(r0, HS), q0 : q0 + qb]
                    q = jnp.concatenate([q] * 8, axis=0)
                    q = jnp.where(sub == h % 8, q, jnp.zeros_like(q))
                    scores = mm(k_s[g], q)
                    if shifted:
                        scores = scores - jnp.max(scores, axis=0, keepdims=True)
                    raised = jnp.exp2(scores * SCALE).astype(BF)
                    out = mm(v_s[h], raised)
                    att_ref[number, pl.ds(r0, HS), q0 : q0 + qb] = (out[:HS] / out[HS : HS + 1]).astype(BF)
                return c

            lax.fori_loop(0, heads, head, 0)

        @pl.when(bound <= SAFE * SAFE)
        def _():
            attend(False)

        @pl.when(jnp.logical_not(bound <= SAFE * SAFE))
        def _():
            attend(True)

        return carry

    lax.fori_loop(0, rows_all // PATCH, patch, 0)


def attention(points, w_qkv):
    rows, width = points.shape
    heads = width // HS
    vm = pl.BlockSpec(memory_space=pltpu.VMEM)
    return pl.pallas_call(
        attention_kernel,
        out_shape=jax.ShapeDtypeStruct((rows // PATCH, width, PATCH), BF),
        in_specs=[vm] * 2,
        out_specs=vm,
        scratch_shapes=[
            pltpu.VMEM((width, width), BF),
            pltpu.VMEM((width, width), BF),
            pltpu.VMEM((width // 128, PATCH, 128), BF),
            pltpu.VMEM((width, PATCH), BF),
            pltpu.VMEM((heads, 2 * HS, PATCH), BF),
        ],
        compiler_params=pltpu.CompilerParams(vmem_limit_bytes=56 * 2**20),
        name="attention",
    )(points, w_qkv)


def tail(points_ref, att_ref, ids_ref, wout_ref, wup_ref, wdown_ref, fin_s, means_ref):
    rows_all = points_ref.shape[0]
    blk = 256
    per = PATCH // blk

    def mlp(i, c):
        rows = pl.ds(pl.multiple_of(i * blk, blk), blk)
        cols = pl.ds(pl.multiple_of(i % per * blk, blk), blk)
        attended = att_ref[i // per, :, cols].T
        middle = points_ref[rows, :].astype(F32) + mm(attended, wout_ref[...])
        normed = normalize(middle).astype(BF)
        hidden = gelu(mm(normed, wup_ref[...])).astype(BF)
        fin_s[rows, :] = (middle + mm(hidden, wdown_ref[...])).astype(BF)
        return c

    lax.fori_loop(0, rows_all // blk, mlp, 0)
    ids = ids_ref[...] - jnp.min(ids_ref[...], axis=1, keepdims=True)
    vb = 128

    def pool(i, c):
        v0 = pl.multiple_of(i * vb, vb)
        marks = jnp.where(lax.broadcasted_iota(I32, (vb, rows_all), 0) + v0 == ids, 1.0, 0.0)
        tally = jnp.sum(marks, axis=1, keepdims=True)
        means_ref[pl.ds(v0, vb), :] = (mm(marks.astype(BF), fin_s[...]) / tally).astype(BF)
        return c

    lax.fori_loop(0, means_ref.shape[0] // vb, pool, 0)


PLANES = 8
SIDE = 32
DEVS = PLANES * SIDE
GROUPS = DEVS // SIDE
MESH = pl.DeviceIdType.MESH


class Links:
    def __init__(self, inner):
        self.inner = inner
        me = lax.axis_index("sp") * inner + lax.axis_index("hd")
        self.plane = lax.div(me, SIDE)
        self.spot = lax.rem(me, SIDE)

    def peer(self, k, j):
        return lax.rem(self.plane + k, PLANES), lax.rem(self.spot + j, SIDE)

    def device(self, plane, spot):
        number = plane * SIDE + spot
        return lax.div(number, self.inner), lax.rem(number, self.inner)

    def signal(self, sem, k, j):
        pl.semaphore_signal(
            sem, inc=1, device_id=self.device(*self.peer(k, j)), device_id_type=MESH
        )

    def greet(self):
        barrier = pltpu.get_barrier_semaphore()

        def up(k, c):
            self.signal(barrier, k, 0)
            return c

        def side(j, c):
            self.signal(barrier, 0, j)
            return c

        lax.fori_loop(1, PLANES, up, 0)
        lax.fori_loop(1, SIDE, side, 0)

    def pass_on(self, ready):
        pl.semaphore_wait(pltpu.get_barrier_semaphore(), PLANES - 1 + SIDE - 1)

        def up(k, c):
            self.signal(ready, k, 0)
            return c

        lax.fori_loop(1, PLANES, up, 0)

    def send(self, streams, g, start):
        def one(s, c):
            plane, spot = self.peer(
                lax.rem(s, PLANES), g * (SIDE // PLANES) + lax.div(s, PLANES)
            )
            for source, by_device, target, sent, got in streams:
                pltpu.make_async_remote_copy(
                    source.at[plane, spot] if by_device else source.at[g, s],
                    target.at[g, s], sent.at[g], got.at[g],
                    device_id=self.device(plane, spot), device_id_type=MESH,
                ).start()
            return c

        lax.fori_loop(start, SIDE, one, 0)

    def keep(self, streams):
        for source, by_device, target, _, _ in streams:
            target[0, 0] = source[self.plane, self.spot] if by_device else source[0, 0]

    def send_all(self, data, pack, ready, extra=None, prepare=None):
        pack(0)
        self.pass_on(ready)
        pack(1)
        self.keep((data,))
        pl.semaphore_wait(ready, PLANES - 1)
        self.send((data,), 0, 1)
        self.send((data,), 1, 0)
        pack(2)
        streams = (data,)
        if extra is not None:
            prepare()
            self.keep((extra,))
            self.send((extra,), 0, 1)
            self.send((extra,), 1, 0)
            streams = (extra, data)

        def more(g, c):
            pack(g + 1)
            self.send(streams, g, 0)
            return c

        lax.fori_loop(2, GROUPS - 1, more, 0)
        self.send(streams, GROUPS - 1, 0)

    def arrived(self, streams, g, count):
        for _, _, target, sent, got in streams:
            held = target.at[g, pl.ds(0, count)]
            pltpu.make_async_copy(held, held, sent.at[g]).wait()
            pltpu.make_async_copy(held, held, got.at[g]).wait()


def rank_rows(target_ref, key_ref, block):
    step = 256
    sub = lax.broadcasted_iota(I32, (DEVS, step), 0)
    lane = lax.broadcasted_iota(I32, (DEVS, step), 1)
    before = jnp.where(sub < lane, 1.0, 0.0).astype(BF)
    count = target_ref.shape[1]

    def ranks(b, seen):
        cols = pl.ds(pl.multiple_of(b * step, step), step)
        owner = lax.shift_right_logical(target_ref[:, cols], block.bit_length() - 1)
        mark = jnp.where(sub == owner, 1.0, 0.0)
        prior = mm(mark.astype(BF), before) + seen
        rank = jnp.sum(mark * prior, axis=0, keepdims=True).astype(I32)
        key_ref[:, cols] = owner * 16 + rank
        return seen + jnp.sum(mark, axis=1, keepdims=True)

    lax.fori_loop(0, count // step, ranks, jnp.zeros((DEVS, 1), F32))


def tag_rows(target_ref, key_ref, acc_ref, block, ranks):
    step = 256
    sub = lax.broadcasted_iota(I32, (DEVS, step), 0)
    nt = (((1,), (1,)), ((), ()))
    width = 256 * len(ranks)
    acc_ref[:, :width] = jnp.zeros((DEVS, width), F32)

    def some(b, c):
        cols = pl.ds(pl.multiple_of(b * step, step), step)
        key = key_ref[:, cols]
        rank = key & 15
        tag = (target_ref[:, cols] & (block - 1)) + 1
        high = lax.shift_right_logical(tag, 4).astype(F32)
        low = (tag & 15).astype(F32)
        marks = jnp.where(sub == lax.shift_right_logical(key, 4), 1.0, 0.0).astype(BF)
        picked = [
            jnp.where(rank == wanted, part, 0.0).astype(BF)
            for wanted in ranks
            for part in (high, low)
        ]
        picked = jnp.concatenate(picked, axis=0)
        acc_ref[:, :width] += lax.dot_general(marks, picked, nt, preferred_element_type=F32)
        return c

    lax.fori_loop(0, target_ref.shape[1] // step, some, 0)
    return [
        (acc_ref[:, i : i + 128] * 16.0 + acc_ref[:, i + 128 : i + 256]).astype(I32)
        for i in range(0, width, 256)
    ]


def packer(links, x_ref, key_ref, send_ref, full):
    width = x_ref.shape[1]
    half = width // 2
    tiles = send_ref.shape[2]
    column = lax.broadcasted_iota(I32, (256, 1), 0)
    slot = lax.shift_right_logical(column, 3)
    rank = column & 7
    first = lax.broadcasted_iota(I32, (SIDE, 8, half), 1) < 4

    def pack(g):
        plane = (links.plane + (slot & (PLANES - 1))) & (PLANES - 1)
        spot = (links.spot + g * (SIDE // PLANES) + lax.shift_right_logical(slot, 3)) & (SIDE - 1)
        base = (plane * SIDE + spot) * 16

        def rows_of(wanted):
            picks = jnp.where(key_ref[...] == wanted, 1.0, 0.0).astype(BF)
            rows = mm(picks, x_ref[...])
            return rows[:, :half].reshape(SIDE, 8, half), rows[:, half:].reshape(SIDE, 8, half)

        if full:
            left, right = rows_of(base + rank)
            send_ref[g, :, 0] = left.astype(BF)
            send_ref[g, :, 1] = right.astype(BF)
        left, right = rows_of(base + full + (rank & 3))
        send_ref[g, :, tiles - 1] = jnp.where(first, left, right).astype(BF)

    return pack


def place_rows(got_ref, g, marks, out_ref, full):
    block, width = out_ref.shape
    half = width // 2
    tiles = got_ref.shape[2]
    chunk = min(block, 512)
    first = lax.broadcasted_iota(I32, (SIDE, 8, half), 1) < 4
    weights = []
    if full:
        left = got_ref[g, :, 0].astype(F32).reshape(256, half)
        right = got_ref[g, :, 1].astype(F32).reshape(256, half)
        weights.append(jnp.concatenate([left, right], axis=1).astype(BF))
    mixed = got_ref[g, :, tiles - 1].astype(F32)
    left = jnp.where(first, mixed, 0.0).reshape(256, half)
    right = jnp.where(first, 0.0, mixed).reshape(256, half)
    weights.append(jnp.concatenate([left, right], axis=1).astype(BF))
    weights = jnp.concatenate(weights, axis=0)
    rows = lax.broadcasted_iota(I32, (chunk, 1), 0) + 1

    def some(i, c):
        r0 = pl.multiple_of(i * chunk, chunk)
        picks = jnp.where(marks == rows + r0, 1.0, 0.0).astype(BF)
        at_rows = pl.ds(r0, chunk)
        out_ref[at_rows, :] = (out_ref[at_rows, :].astype(F32) + mm(picks, weights)).astype(BF)
        return c

    lax.fori_loop(0, block // chunk, some, 0)


def spread_kernel(
    full, inner, voxels, x_ref, target_ref, owner_ref, out_ref, key_out, marks_out,
    key_s, acc_s, send_s, tags_s, got_s, seen_s, d_send, d_recv, t_send, t_recv, ready,
):
    links = Links(inner)
    links.greet()
    block = out_ref.shape[0]
    rank_rows(target_ref, key_s, block)

    def prepare():
        rank_rows(owner_ref, key_out, voxels)
        eight = lax.broadcasted_iota(I32, (128, 1), 0) & 7
        four = eight & 3
        first, second = tag_rows(target_ref, key_s, acc_s, block, (eight, full + four))
        (third,) = tag_rows(owner_ref, key_out, acc_s, voxels, (four,))
        lane = lax.shift_right_logical(lax.broadcasted_iota(I32, (DEVS, 128), 1), 3)
        owner = lax.broadcasted_iota(I32, (DEVS, 1), 0)
        k = (lax.shift_right_logical(owner, 5) - links.plane) & (PLANES - 1)
        j = ((owner & (SIDE - 1)) - links.spot) & (SIDE - 1)
        slot = (j & 1) * 8 + k
        tags = jnp.where(lane == slot, first + 4096 * second, 0)
        tags = jnp.where(lane == (slot + 8) & 15, third, tags)
        tags_s[...] = tags.reshape(PLANES, SIDE, 1, 128)
        out_ref[...] = jnp.zeros_like(out_ref)

    extra = (tags_s, True, seen_s, t_send, t_recv)
    data = (send_s, False, got_s, d_send, d_recv)
    links.send_all(data, packer(links, x_ref, key_s, send_s, full), ready, extra, prepare)
    streams = (extra, data)
    low = lax.broadcasted_iota(I32, (1, 128), 1) < 64

    def land(g, count):
        links.arrived(streams, g, count)
        points, later = [], []
        for part in range(2):
            a = jnp.sum(seen_s[g, part * 16 : part * 16 + 8], axis=0)
            b = jnp.sum(seen_s[g, part * 16 + 8 : part * 16 + 16], axis=0)
            points.append(jnp.where(low, a, b))
            other = jnp.where(low, b, a)
            later.append(jnp.concatenate([other[:, 64:], other[:, :64]], axis=1))
        points = jnp.concatenate(points, axis=1)
        marks_out[g] = jnp.concatenate(later, axis=1)
        marks = jnp.concatenate(
            [points & 4095, lax.shift_right_logical(points, 12)], axis=1
        )
        place_rows(got_s, g, marks, out_ref, full)

    land(0, SIDE - 1)

    def more(g, c):
        land(g, SIDE)
        return c

    lax.fori_loop(1, GROUPS, more, 0)


def spread(x, target, owner, capacity, inner):
    count, width = x.shape
    voxels = owner.shape[1]
    vm = pl.BlockSpec(memory_space=pltpu.VMEM)
    data = pltpu.VMEM((PLANES, SIDE, capacity // 4, 8, width // 2), BF)
    tags = pltpu.VMEM((PLANES, SIDE, 1, 128), I32)
    return pl.pallas_call(
        functools.partial(spread_kernel, capacity - 4, inner, voxels),
        out_shape=(
            jax.ShapeDtypeStruct((count, width), BF),
            jax.ShapeDtypeStruct((1, voxels), I32),
            jax.ShapeDtypeStruct((PLANES, 1, 256), I32),
        ),
        in_specs=[vm] * 3,
        out_specs=[vm] * 3,
        scratch_shapes=[
            pltpu.VMEM((1, count), I32), pltpu.VMEM((DEVS, 512), F32), data, tags, data, tags
        ]
        + [pltpu.SemaphoreType.DMA((PLANES,))] * 4
        + [pltpu.SemaphoreType.REGULAR],
        compiler_params=pltpu.CompilerParams(
            collective_id=1, has_side_effects=True, vmem_limit_bytes=56 * 2**20
        ),
        name="spread",
    )(x, target, owner)


def gather_kernel(
    inner, points_ref, att_ref, ids_ref, wout_ref, wup_ref, wdown_ref, key_ref, marks_ref, out_ref,
    fin_s, x_ref, send_s, got_s, d_send, d_recv, ready,
):
    links = Links(inner)
    links.greet()
    tail(points_ref, att_ref, ids_ref, wout_ref, wup_ref, wdown_ref, fin_s, x_ref)
    out_ref[...] = jnp.zeros_like(out_ref)
    data = (send_s, False, got_s, d_send, d_recv)
    links.send_all(data, packer(links, x_ref, key_ref, send_s, 0), ready)
    streams = (data,)

    def land(g, count):
        links.arrived(streams, g, count)
        place_rows(got_s, g, marks_ref[g], out_ref, 0)

    land(0, SIDE - 1)

    def more(g, c):
        land(g, SIDE)
        return c

    lax.fori_loop(1, GROUPS, more, 0)


def gather(points, att, ids, w_out, w_up, w_down, key, marks, inner):
    width = points.shape[1]
    count = key.shape[1]
    vm = pl.BlockSpec(memory_space=pltpu.VMEM)
    data = pltpu.VMEM((PLANES, SIDE, 1, 8, width // 2), BF)
    return pl.pallas_call(
        functools.partial(gather_kernel, inner),
        out_shape=jax.ShapeDtypeStruct((count, width), BF),
        in_specs=[vm] * 8,
        out_specs=vm,
        scratch_shapes=[pltpu.VMEM(points.shape, BF), pltpu.VMEM((count, width), BF), data, data]
        + [pltpu.SemaphoreType.DMA((PLANES,))] * 2
        + [pltpu.SemaphoreType.REGULAR],
        compiler_params=pltpu.CompilerParams(
            collective_id=2, has_side_effects=True, vmem_limit_bytes=56 * 2**20
        ),
        name="gather",
    )(points, att, ids, w_out, w_up, w_down, key, marks)


def finish_kernel(x_ref, w_ref, out_ref):
    block = 128

    def some(i, c):
        rows = pl.ds(pl.multiple_of(i * block, block), block)
        out_ref[rows, :] = gelu(normalize(mm(x_ref[rows, :], w_ref[...]))).astype(BF)
        return c

    lax.fori_loop(0, x_ref.shape[0] // block, some, 0)


def finish(x, w):
    vm = pl.BlockSpec(memory_space=pltpu.VMEM)
    return pl.pallas_call(
        finish_kernel,
        out_shape=jax.ShapeDtypeStruct((x.shape[0], w.shape[1]), BF),
        in_specs=[vm] * 2,
        out_specs=vm,
        name="finish",
    )(x, w)


def per_device(features, point_dest, cluster, owner_row, w_qkv, w_out, w_up, w_down, w_pool):
    inner = lax.axis_size("hd")
    points, key, marks = spread(
        features, point_dest.reshape(1, -1), owner_row.reshape(1, -1), 12, inner
    )
    att = attention(points, w_qkv)
    placed = gather(
        points, att, cluster.reshape(1, -1), w_out, w_up, w_down, key, marks, inner
    )
    return finish(placed, w_pool)


def solution(mesh):
    rows = P(("sp", "hd"), None)
    line = P(("sp", "hd"))
    return jax.shard_map(
        per_device,
        mesh=mesh,
        in_specs=(rows, line, line, line, P(), P(), P(), P(), P()),
        out_specs=rows,
        check_vma=False,
    )
```

```python
import functools
import jax
import jax.numpy as jnp
from jax import lax
from jax.experimental import pallas as pl
from jax.experimental.pallas import tpu as pltpu
from jax.sharding import PartitionSpec as P

BF = jnp.bfloat16
F32 = jnp.float32
I32 = jnp.int32
HS = 16
PATCH = 1024
EPSILON = 1e-05
LOG2E = 1.4426950408889634
SCALE = HS ** (-0.5) * LOG2E
SAFE = 100.0


def normalize(values):
    center = jnp.mean(values, axis=-1, keepdims=True)
    shifted = values - center
    spread = jnp.mean(shifted * shifted, axis=-1, keepdims=True)
    return shifted * lax.rsqrt(spread + EPSILON)


def gelu(values):
    return 0.5 * values * (1.0 + lax.erf(values * (0.5**0.5)))


def mm(a, b):
    return jnp.dot(a, b, preferred_element_type=F32)


def attention_kernel(
    points_ref, wqkv_ref, att_ref, wq_s, wv_s, k_s, q_s, v_s,
):
    rows_all, width = points_ref.shape
    heads = width // HS
    blk = 256
    groups = width // 128
    wq_s[...] = wqkv_ref[0].T
    wv_s[...] = wqkv_ref[2].T
    v_s[:, HS:, :] = jnp.ones((heads, HS, PATCH), BF)
    head_mask = (
        lax.broadcasted_iota(I32, (width, 128), 0) // HS
        == lax.broadcasted_iota(I32, (width, 128), 1)
    ).astype(BF)

    def patch(number, carry):
        base = number * PATCH

        def project(i, bound):
            qmax, kmax = bound
            r0 = pl.multiple_of(i * blk, blk)
            x = points_ref[pl.ds(pl.multiple_of(base + r0, blk), blk), :].astype(F32)
            normed = normalize(x).astype(BF)
            keys = mm(normed, wqkv_ref[1])
            for g in range(groups):
                k_s[g, pl.ds(r0, blk), :] = keys[:, g * 128 : (g + 1) * 128].astype(BF)
            nt = (((1,), (1,)), ((), ()))
            queries = lax.dot_general(wq_s[...], normed, nt, preferred_element_type=F32)
            values = lax.dot_general(wv_s[...], normed, nt, preferred_element_type=F32)
            q_s[:, pl.ds(r0, blk)] = queries.astype(BF)
            v_s[:, 0:HS, pl.ds(r0, blk)] = values.astype(BF).reshape(heads, HS, blk)
            knorm = mm((keys * keys).astype(BF), head_mask)
            qnorm = jnp.sum((queries * queries).reshape(heads, HS, blk), axis=1)
            return (jnp.maximum(qmax, qnorm), jnp.maximum(kmax, jnp.max(knorm, axis=0, keepdims=True)))

        qmax, kmax = lax.fori_loop(
            0, PATCH // blk, project,
            (jnp.zeros((heads, blk), F32), jnp.zeros((1, 128), F32)),
            unroll=2,
        )
        bound = 1.05 * SCALE * SCALE * jnp.max(qmax) * jnp.max(kmax)
        qb = 512
        sub = lax.broadcasted_iota(I32, (128, qb), 0) // HS

        def attend(shifted):
            def head(h, c):
                g = h // 8
                r0 = pl.multiple_of(h * HS, HS)
                for q0 in range(0, PATCH, qb):
                    q = q_s[pl.ds(r0, HS), q0 : q0 + qb]
                    q = jnp.concatenate([q] * 8, axis=0)
                    q = jnp.where(sub == h % 8, q, jnp.zeros_like(q))
                    scores = mm(k_s[g], q)
                    if shifted:
                        scores = scores - jnp.max(scores, axis=0, keepdims=True)
                    raised = jnp.exp2(scores * SCALE).astype(BF)
                    out = mm(v_s[h], raised)
                    att_ref[number, pl.ds(r0, HS), q0 : q0 + qb] = (out[:HS] / out[HS : HS + 1]).astype(BF)
                return c

            lax.fori_loop(0, heads, head, 0, unroll=1 if shifted else 2)

        @pl.when(bound <= SAFE * SAFE)
        def _():
            attend(False)

        @pl.when(jnp.logical_not(bound <= SAFE * SAFE))
        def _():
            attend(True)

        return carry

    lax.fori_loop(0, rows_all // PATCH, patch, 0)


def attention(points, w_qkv):
    rows, width = points.shape
    heads = width // HS
    vm = pl.BlockSpec(memory_space=pltpu.VMEM)
    return pl.pallas_call(
        attention_kernel,
        out_shape=jax.ShapeDtypeStruct((rows // PATCH, width, PATCH), BF),
        in_specs=[vm] * 2,
        out_specs=vm,
        scratch_shapes=[
            pltpu.VMEM((width, width), BF),
            pltpu.VMEM((width, width), BF),
            pltpu.VMEM((width // 128, PATCH, 128), BF),
            pltpu.VMEM((width, PATCH), BF),
            pltpu.VMEM((heads, 2 * HS, PATCH), BF),
        ],
        compiler_params=pltpu.CompilerParams(vmem_limit_bytes=56 * 2**20),
        name="attention",
    )(points, w_qkv)


def tail(points_ref, att_ref, ids_ref, wout_ref, wup_ref, wdown_ref, fin_s, means_ref):
    rows_all = points_ref.shape[0]
    blk = 256
    per = PATCH // blk

    def mlp(i, c):
        rows = pl.ds(pl.multiple_of(i * blk, blk), blk)
        cols = pl.ds(pl.multiple_of(i % per * blk, blk), blk)
        attended = att_ref[i // per, :, cols].T
        middle = points_ref[rows, :].astype(F32) + mm(attended, wout_ref[...])
        normed = normalize(middle).astype(BF)
        hidden = gelu(mm(normed, wup_ref[...])).astype(BF)
        fin_s[rows, :] = (middle + mm(hidden, wdown_ref[...])).astype(BF)
        return c

    lax.fori_loop(0, rows_all // blk, mlp, 0, unroll=2)
    ids = ids_ref[...] - jnp.min(ids_ref[...], axis=1, keepdims=True)
    vb = 128

    def pool(i, c):
        v0 = pl.multiple_of(i * vb, vb)
        marks = jnp.where(lax.broadcasted_iota(I32, (vb, rows_all), 0) + v0 == ids, 1.0, 0.0)
        tally = jnp.sum(marks, axis=1, keepdims=True)
        means_ref[pl.ds(v0, vb), :] = (mm(marks.astype(BF), fin_s[...]) / tally).astype(BF)
        return c

    lax.fori_loop(0, means_ref.shape[0] // vb, pool, 0, unroll=2)


PLANES = 8
SIDE = 32
DEVS = PLANES * SIDE
GROUPS = DEVS // SIDE
MESH = pl.DeviceIdType.MESH


class Links:
    def __init__(self, inner):
        self.inner = inner
        me = lax.axis_index("sp") * inner + lax.axis_index("hd")
        self.plane = lax.div(me, SIDE)
        self.spot = lax.rem(me, SIDE)

    def peer(self, k, j):
        return lax.rem(self.plane + k, PLANES), lax.rem(self.spot + j, SIDE)

    def device(self, plane, spot):
        number = plane * SIDE + spot
        return lax.div(number, self.inner), lax.rem(number, self.inner)

    def signal(self, sem, k, j):
        pl.semaphore_signal(
            sem, inc=1, device_id=self.device(*self.peer(k, j)), device_id_type=MESH
        )

    def greet(self):
        barrier = pltpu.get_barrier_semaphore()

        def up(k, c):
            self.signal(barrier, k, 0)
            return c

        def side(j, c):
            self.signal(barrier, 0, j)
            return c

        lax.fori_loop(1, PLANES, up, 0)
        lax.fori_loop(1, SIDE, side, 0)

    def pass_on(self, ready):
        pl.semaphore_wait(pltpu.get_barrier_semaphore(), PLANES - 1 + SIDE - 1)

        def up(k, c):
            self.signal(ready, k, 0)
            return c

        lax.fori_loop(1, PLANES, up, 0)

    def send(self, streams, g, start):
        def one(s, c):
            plane, spot = self.peer(
                lax.rem(s, PLANES), g * (SIDE // PLANES) + lax.div(s, PLANES)
            )
            for source, by_device, target, sent, got in streams:
                pltpu.make_async_remote_copy(
                    source.at[plane, spot] if by_device else source.at[g, s],
                    target.at[g, s], sent.at[g], got.at[g],
                    device_id=self.device(plane, spot), device_id_type=MESH,
                ).start()
            return c

        lax.fori_loop(start, SIDE, one, 0)

    def keep(self, streams):
        for source, by_device, target, _, _ in streams:
            target[0, 0] = source[self.plane, self.spot] if by_device else source[0, 0]

    def send_all(self, data, pack, ready, extra=None, prepare=None):
        pack(0)
        self.pass_on(ready)
        pack(1)
        self.keep((data,))
        pl.semaphore_wait(ready, PLANES - 1)
        self.send((data,), 0, 1)
        self.send((data,), 1, 0)
        pack(2)
        streams = (data,)
        if extra is not None:
            prepare()
            self.keep((extra,))
            self.send((extra,), 0, 1)
            self.send((extra,), 1, 0)
            streams = (extra, data)

        def more(g, c):
            pack(g + 1)
            self.send(streams, g, 0)
            return c

        lax.fori_loop(2, GROUPS - 1, more, 0)
        self.send(streams, GROUPS - 1, 0)

    def arrived(self, streams, g, count):
        for _, _, target, sent, got in streams:
            held = target.at[g, pl.ds(0, count)]
            pltpu.make_async_copy(held, held, sent.at[g]).wait()
            pltpu.make_async_copy(held, held, got.at[g]).wait()


def rank_rows(target_ref, key_ref, block):
    step = 256
    sub = lax.broadcasted_iota(I32, (DEVS, step), 0)
    lane = lax.broadcasted_iota(I32, (DEVS, step), 1)
    before = jnp.where(sub < lane, 1.0, 0.0).astype(BF)
    count = target_ref.shape[1]

    def ranks(b, seen):
        cols = pl.ds(pl.multiple_of(b * step, step), step)
        owner = lax.shift_right_logical(target_ref[:, cols], block.bit_length() - 1)
        mark = jnp.where(sub == owner, 1.0, 0.0)
        prior = mm(mark.astype(BF), before) + seen
        rank = jnp.sum(mark * prior, axis=0, keepdims=True).astype(I32)
        key_ref[:, cols] = owner * 16 + rank
        return seen + jnp.sum(mark, axis=1, keepdims=True)

    lax.fori_loop(0, count // step, ranks, jnp.zeros((DEVS, 1), F32))


def tag_rows(target_ref, key_ref, acc_ref, block, ranks):
    step = 256
    sub = lax.broadcasted_iota(I32, (DEVS, step), 0)
    nt = (((1,), (1,)), ((), ()))
    width = 256 * len(ranks)
    acc_ref[:, :width] = jnp.zeros((DEVS, width), F32)

    def some(b, c):
        cols = pl.ds(pl.multiple_of(b * step, step), step)
        key = key_ref[:, cols]
        rank = key & 15
        tag = (target_ref[:, cols] & (block - 1)) + 1
        high = lax.shift_right_logical(tag, 4).astype(F32)
        low = (tag & 15).astype(F32)
        marks = jnp.where(sub == lax.shift_right_logical(key, 4), 1.0, 0.0).astype(BF)
        picked = [
            jnp.where(rank == wanted, part, 0.0).astype(BF)
            for wanted in ranks
            for part in (high, low)
        ]
        picked = jnp.concatenate(picked, axis=0)
        acc_ref[:, :width] += lax.dot_general(marks, picked, nt, preferred_element_type=F32)
        return c

    lax.fori_loop(0, target_ref.shape[1] // step, some, 0)
    return [
        (acc_ref[:, i : i + 128] * 16.0 + acc_ref[:, i + 128 : i + 256]).astype(I32)
        for i in range(0, width, 256)
    ]


def packer(links, x_ref, key_ref, send_ref, full):
    width = x_ref.shape[1]
    half = width // 2
    tiles = send_ref.shape[2]
    column = lax.broadcasted_iota(I32, (256, 1), 0)
    slot = lax.shift_right_logical(column, 3)
    rank = column & 7
    first = lax.broadcasted_iota(I32, (SIDE, 8, half), 1) < 4

    def pack(g):
        plane = (links.plane + (slot & (PLANES - 1))) & (PLANES - 1)
        spot = (links.spot + g * (SIDE // PLANES) + lax.shift_right_logical(slot, 3)) & (SIDE - 1)
        base = (plane * SIDE + spot) * 16

        def rows_of(wanted):
            picks = jnp.where(key_ref[...] == wanted, 1.0, 0.0).astype(BF)
            rows = mm(picks, x_ref[...])
            return rows[:, :half].reshape(SIDE, 8, half), rows[:, half:].reshape(SIDE, 8, half)

        if full:
            left, right = rows_of(base + rank)
            send_ref[g, :, 0] = left.astype(BF)
            send_ref[g, :, 1] = right.astype(BF)
        left, right = rows_of(base + full + (rank & 3))
        send_ref[g, :, tiles - 1] = jnp.where(first, left, right).astype(BF)

    return pack


def place_rows(got_ref, g, marks, out_ref, full):
    block, width = out_ref.shape
    half = width // 2
    tiles = got_ref.shape[2]
    chunk = min(block, 512)
    first = lax.broadcasted_iota(I32, (SIDE, 8, half), 1) < 4
    weights = []
    if full:
        left = got_ref[g, :, 0].astype(F32).reshape(256, half)
        right = got_ref[g, :, 1].astype(F32).reshape(256, half)
        weights.append(jnp.concatenate([left, right], axis=1).astype(BF))
    mixed = got_ref[g, :, tiles - 1].astype(F32)
    left = jnp.where(first, mixed, 0.0).reshape(256, half)
    right = jnp.where(first, 0.0, mixed).reshape(256, half)
    weights.append(jnp.concatenate([left, right], axis=1).astype(BF))
    weights = jnp.concatenate(weights, axis=0)
    rows = lax.broadcasted_iota(I32, (chunk, 1), 0) + 1

    def some(i, c):
        r0 = pl.multiple_of(i * chunk, chunk)
        picks = jnp.where(marks == rows + r0, 1.0, 0.0).astype(BF)
        at_rows = pl.ds(r0, chunk)
        out_ref[at_rows, :] = (out_ref[at_rows, :].astype(F32) + mm(picks, weights)).astype(BF)
        return c

    lax.fori_loop(0, block // chunk, some, 0)


def spread_kernel(
    full, inner, voxels, x_ref, target_ref, owner_ref, out_ref, key_out, marks_out,
    key_s, acc_s, send_s, tags_s, got_s, seen_s, d_send, d_recv, t_send, t_recv, ready,
):
    links = Links(inner)
    links.greet()
    block = out_ref.shape[0]
    rank_rows(target_ref, key_s, block)

    def prepare():
        rank_rows(owner_ref, key_out, voxels)
        eight = lax.broadcasted_iota(I32, (128, 1), 0) & 7
        four = eight & 3
        first, second = tag_rows(target_ref, key_s, acc_s, block, (eight, full + four))
        (third,) = tag_rows(owner_ref, key_out, acc_s, voxels, (four,))
        lane = lax.shift_right_logical(lax.broadcasted_iota(I32, (DEVS, 128), 1), 3)
        owner = lax.broadcasted_iota(I32, (DEVS, 1), 0)
        k = (lax.shift_right_logical(owner, 5) - links.plane) & (PLANES - 1)
        j = ((owner & (SIDE - 1)) - links.spot) & (SIDE - 1)
        slot = (j & 1) * 8 + k
        tags = jnp.where(lane == slot, first + 4096 * second, 0)
        tags = jnp.where(lane == (slot + 8) & 15, third, tags)
        tags_s[...] = tags.reshape(PLANES, SIDE, 1, 128)
        out_ref[...] = jnp.zeros_like(out_ref)

    extra = (tags_s, True, seen_s, t_send, t_recv)
    data = (send_s, False, got_s, d_send, d_recv)
    links.send_all(data, packer(links, x_ref, key_s, send_s, full), ready, extra, prepare)
    streams = (extra, data)
    low = lax.broadcasted_iota(I32, (1, 128), 1) < 64

    def land(g, count):
        links.arrived(streams, g, count)
        points, later = [], []
        for part in range(2):
            a = jnp.sum(seen_s[g, part * 16 : part * 16 + 8], axis=0)
            b = jnp.sum(seen_s[g, part * 16 + 8 : part * 16 + 16], axis=0)
            points.append(jnp.where(low, a, b))
            other = jnp.where(low, b, a)
            later.append(jnp.concatenate([other[:, 64:], other[:, :64]], axis=1))
        points = jnp.concatenate(points, axis=1)
        marks_out[g] = jnp.concatenate(later, axis=1)
        marks = jnp.concatenate(
            [points & 4095, lax.shift_right_logical(points, 12)], axis=1
        )
        place_rows(got_s, g, marks, out_ref, full)

    land(0, SIDE - 1)

    def more(g, c):
        land(g, SIDE)
        return c

    lax.fori_loop(1, GROUPS, more, 0)


def spread(x, target, owner, capacity, inner):
    count, width = x.shape
    voxels = owner.shape[1]
    vm = pl.BlockSpec(memory_space=pltpu.VMEM)
    data = pltpu.VMEM((PLANES, SIDE, capacity // 4, 8, width // 2), BF)
    tags = pltpu.VMEM((PLANES, SIDE, 1, 128), I32)
    return pl.pallas_call(
        functools.partial(spread_kernel, capacity - 4, inner, voxels),
        out_shape=(
            jax.ShapeDtypeStruct((count, width), BF),
            jax.ShapeDtypeStruct((1, voxels), I32),
            jax.ShapeDtypeStruct((PLANES, 1, 256), I32),
        ),
        in_specs=[vm] * 3,
        out_specs=[vm] * 3,
        scratch_shapes=[
            pltpu.VMEM((1, count), I32), pltpu.VMEM((DEVS, 512), F32), data, tags, data, tags
        ]
        + [pltpu.SemaphoreType.DMA((PLANES,))] * 4
        + [pltpu.SemaphoreType.REGULAR],
        compiler_params=pltpu.CompilerParams(
            collective_id=1, has_side_effects=True, vmem_limit_bytes=56 * 2**20
        ),
        name="spread",
    )(x, target, owner)


def gather_kernel(
    inner, points_ref, att_ref, ids_ref, wout_ref, wup_ref, wdown_ref, key_ref, marks_ref, out_ref,
    fin_s, x_ref, send_s, got_s, d_send, d_recv, ready,
):
    links = Links(inner)
    links.greet()
    tail(points_ref, att_ref, ids_ref, wout_ref, wup_ref, wdown_ref, fin_s, x_ref)
    out_ref[...] = jnp.zeros_like(out_ref)
    data = (send_s, False, got_s, d_send, d_recv)
    links.send_all(data, packer(links, x_ref, key_ref, send_s, 0), ready)
    streams = (data,)

    def land(g, count):
        links.arrived(streams, g, count)
        place_rows(got_s, g, marks_ref[g], out_ref, 0)

    land(0, SIDE - 1)

    def more(g, c):
        land(g, SIDE)
        return c

    lax.fori_loop(1, GROUPS, more, 0)


def gather(points, att, ids, w_out, w_up, w_down, key, marks, inner):
    width = points.shape[1]
    count = key.shape[1]
    vm = pl.BlockSpec(memory_space=pltpu.VMEM)
    data = pltpu.VMEM((PLANES, SIDE, 1, 8, width // 2), BF)
    return pl.pallas_call(
        functools.partial(gather_kernel, inner),
        out_shape=jax.ShapeDtypeStruct((count, width), BF),
        in_specs=[vm] * 8,
        out_specs=vm,
        scratch_shapes=[pltpu.VMEM(points.shape, BF), pltpu.VMEM((count, width), BF), data, data]
        + [pltpu.SemaphoreType.DMA((PLANES,))] * 2
        + [pltpu.SemaphoreType.REGULAR],
        compiler_params=pltpu.CompilerParams(
            collective_id=2, has_side_effects=True, vmem_limit_bytes=56 * 2**20
        ),
        name="gather",
    )(points, att, ids, w_out, w_up, w_down, key, marks)


def finish_kernel(x_ref, w_ref, out_ref):
    block = 128

    def some(i, c):
        rows = pl.ds(pl.multiple_of(i * block, block), block)
        out_ref[rows, :] = gelu(normalize(mm(x_ref[rows, :], w_ref[...]))).astype(BF)
        return c

    lax.fori_loop(0, x_ref.shape[0] // block, some, 0)


def finish(x, w):
    vm = pl.BlockSpec(memory_space=pltpu.VMEM)
    return pl.pallas_call(
        finish_kernel,
        out_shape=jax.ShapeDtypeStruct((x.shape[0], w.shape[1]), BF),
        in_specs=[vm] * 2,
        out_specs=vm,
        name="finish",
    )(x, w)


def per_device(features, point_dest, cluster, owner_row, w_qkv, w_out, w_up, w_down, w_pool):
    inner = lax.axis_size("hd")
    points, key, marks = spread(
        features, point_dest.reshape(1, -1), owner_row.reshape(1, -1), 12, inner
    )
    att = attention(points, w_qkv)
    placed = gather(
        points, att, cluster.reshape(1, -1), w_out, w_up, w_down, key, marks, inner
    )
    return finish(placed, w_pool)


def solution(mesh):
    rows = P(("sp", "hd"), None)
    line = P(("sp", "hd"))
    return jax.shard_map(
        per_device,
        mesh=mesh,
        in_specs=(rows, line, line, line, P(), P(), P(), P(), P()),
        out_specs=rows,
        check_vma=False,
    )
```

```python
import functools
import jax
import jax.numpy as jnp
from jax import lax
from jax.experimental import pallas as pl
from jax.experimental.pallas import tpu as pltpu
from jax.sharding import PartitionSpec as P

BF = jnp.bfloat16
F32 = jnp.float32
I32 = jnp.int32
HS = 16
PATCH = 1024
EPSILON = 1e-05
LOG2E = 1.4426950408889634
SCALE = HS ** (-0.5) * LOG2E
SAFE = 100.0


def normalize(values):
    center = jnp.mean(values, axis=-1, keepdims=True)
    shifted = values - center
    spread = jnp.mean(shifted * shifted, axis=-1, keepdims=True)
    return shifted * lax.rsqrt(spread + EPSILON)


def gelu(values):
    return 0.5 * values * (1.0 + lax.erf(values * (0.5**0.5)))


def mm(a, b):
    return jnp.dot(a, b, preferred_element_type=F32)


def attention_kernel(
    points_ref, wqkv_ref, att_ref, wq_s, wv_s, k_s, q_s, v_s,
):
    rows_all, width = points_ref.shape
    heads = width // HS
    blk = 256
    groups = width // 128
    wq_s[...] = wqkv_ref[0].T
    wv_s[...] = wqkv_ref[2].T
    v_s[:, HS:, :] = jnp.ones((heads, HS, PATCH), BF)
    head_mask = (
        lax.broadcasted_iota(I32, (width, 128), 0) // HS
        == lax.broadcasted_iota(I32, (width, 128), 1)
    ).astype(BF)

    def patch(number, carry):
        base = number * PATCH

        def project(i, bound):
            qmax, kmax = bound
            r0 = pl.multiple_of(i * blk, blk)
            x = points_ref[pl.ds(pl.multiple_of(base + r0, blk), blk), :].astype(F32)
            normed = normalize(x).astype(BF)
            keys = mm(normed, wqkv_ref[1])
            for g in range(groups):
                k_s[g, pl.ds(r0, blk), :] = keys[:, g * 128 : (g + 1) * 128].astype(BF)
            nt = (((1,), (1,)), ((), ()))
            queries = lax.dot_general(wq_s[...], normed, nt, preferred_element_type=F32)
            values = lax.dot_general(wv_s[...], normed, nt, preferred_element_type=F32)
            q_s[:, pl.ds(r0, blk)] = queries.astype(BF)
            v_s[:, 0:HS, pl.ds(r0, blk)] = values.astype(BF).reshape(heads, HS, blk)
            knorm = mm((keys * keys).astype(BF), head_mask)
            qnorm = jnp.sum((queries * queries).reshape(heads, HS, blk), axis=1)
            return (jnp.maximum(qmax, qnorm), jnp.maximum(kmax, jnp.max(knorm, axis=0, keepdims=True)))

        qmax, kmax = lax.fori_loop(
            0, PATCH // blk, project,
            (jnp.zeros((heads, blk), F32), jnp.zeros((1, 128), F32)),
            unroll=2,
        )
        bound = 1.05 * SCALE * SCALE * jnp.max(qmax) * jnp.max(kmax)
        qb = 512
        sub = lax.broadcasted_iota(I32, (128, qb), 0) // HS

        def attend(shifted):
            def head(h, c):
                g = h // 8
                r0 = pl.multiple_of(h * HS, HS)
                for q0 in range(0, PATCH, qb):
                    q = q_s[pl.ds(r0, HS), q0 : q0 + qb]
                    q = jnp.concatenate([q] * 8, axis=0)
                    q = jnp.where(sub == h % 8, q, jnp.zeros_like(q))
                    scores = mm(k_s[g], q)
                    if shifted:
                        scores = scores - jnp.max(scores, axis=0, keepdims=True)
                    raised = jnp.exp2(scores * SCALE).astype(BF)
                    out = mm(v_s[h], raised)
                    att_ref[number, pl.ds(r0, HS), q0 : q0 + qb] = (out[:HS] / out[HS : HS + 1]).astype(BF)
                return c

            lax.fori_loop(0, heads, head, 0, unroll=1 if shifted else 2)

        @pl.when(bound <= SAFE * SAFE)
        def _():
            attend(False)

        @pl.when(jnp.logical_not(bound <= SAFE * SAFE))
        def _():
            attend(True)

        return carry

    lax.fori_loop(0, rows_all // PATCH, patch, 0)


def attention(points, w_qkv):
    rows, width = points.shape
    heads = width // HS
    vm = pl.BlockSpec(memory_space=pltpu.VMEM)
    return pl.pallas_call(
        attention_kernel,
        out_shape=jax.ShapeDtypeStruct((rows // PATCH, width, PATCH), BF),
        in_specs=[vm] * 2,
        out_specs=vm,
        scratch_shapes=[
            pltpu.VMEM((width, width), BF),
            pltpu.VMEM((width, width), BF),
            pltpu.VMEM((width // 128, PATCH, 128), BF),
            pltpu.VMEM((width, PATCH), BF),
            pltpu.VMEM((heads, 2 * HS, PATCH), BF),
        ],
        compiler_params=pltpu.CompilerParams(vmem_limit_bytes=56 * 2**20),
        name="attention",
    )(points, w_qkv)


def tail(points_ref, att_ref, ids_ref, wout_ref, wup_ref, wdown_ref, fin_s, means_ref):
    rows_all = points_ref.shape[0]
    blk = 256
    per = PATCH // blk

    def mlp(i, c):
        rows = pl.ds(pl.multiple_of(i * blk, blk), blk)
        cols = pl.ds(pl.multiple_of(i % per * blk, blk), blk)
        attended = att_ref[i // per, :, cols].T
        middle = points_ref[rows, :].astype(F32) + mm(attended, wout_ref[...])
        normed = normalize(middle).astype(BF)
        hidden = gelu(mm(normed, wup_ref[...])).astype(BF)
        fin_s[rows, :] = (middle + mm(hidden, wdown_ref[...])).astype(BF)
        return c

    lax.fori_loop(0, rows_all // blk, mlp, 0, unroll=2)
    ids = ids_ref[...] - jnp.min(ids_ref[...], axis=1, keepdims=True)
    vb = 128

    def pool(i, c):
        v0 = pl.multiple_of(i * vb, vb)
        marks = jnp.where(lax.broadcasted_iota(I32, (vb, rows_all), 0) + v0 == ids, 1.0, 0.0)
        tally = jnp.sum(marks, axis=1, keepdims=True)
        means_ref[pl.ds(v0, vb), :] = (mm(marks.astype(BF), fin_s[...]) / tally).astype(BF)
        return c

    lax.fori_loop(0, means_ref.shape[0] // vb, pool, 0, unroll=2)


PLANES = 8
SIDE = 32
DEVS = PLANES * SIDE
GROUPS = DEVS // SIDE
MESH = pl.DeviceIdType.MESH


class Links:
    def __init__(self, inner):
        self.inner = inner
        me = lax.axis_index("sp") * inner + lax.axis_index("hd")
        self.plane = lax.div(me, SIDE)
        self.spot = lax.rem(me, SIDE)

    def peer(self, k, j):
        return lax.rem(self.plane + k, PLANES), lax.rem(self.spot + j, SIDE)

    def device(self, plane, spot):
        number = plane * SIDE + spot
        return lax.div(number, self.inner), lax.rem(number, self.inner)

    def signal(self, sem, k, j):
        pl.semaphore_signal(
            sem, inc=1, device_id=self.device(*self.peer(k, j)), device_id_type=MESH
        )

    def greet(self):
        barrier = pltpu.get_barrier_semaphore()

        def up(k, c):
            self.signal(barrier, k, 0)
            return c

        def side(j, c):
            self.signal(barrier, 0, j)
            return c

        lax.fori_loop(1, PLANES, up, 0)
        lax.fori_loop(1, SIDE, side, 0)

    def pass_on(self, ready):
        pl.semaphore_wait(pltpu.get_barrier_semaphore(), PLANES - 1 + SIDE - 1)

        def up(k, c):
            self.signal(ready, k, 0)
            return c

        lax.fori_loop(1, PLANES, up, 0)

    def send(self, streams, g, start):
        def one(s, c):
            b = lax.div(s, PLANES)
            plane, spot = self.peer(
                lax.rem(s, PLANES), PLANES * b + lax.rem(g + 2 * b, PLANES)
            )
            for source, by_device, target, sent, got in streams:
                pltpu.make_async_remote_copy(
                    source.at[plane, spot] if by_device else source.at[g, s],
                    target.at[g, s], sent.at[g], got.at[g],
                    device_id=self.device(plane, spot), device_id_type=MESH,
                ).start()
            return c

        lax.fori_loop(start, SIDE, one, 0)

    def keep(self, streams):
        for source, by_device, target, _, _ in streams:
            target[0, 0] = source[self.plane, self.spot] if by_device else source[0, 0]

    def send_all(self, data, pack, ready, extra=None, prepare=None):
        pack(0)
        self.pass_on(ready)
        pack(1)
        self.keep((data,))
        pl.semaphore_wait(ready, PLANES - 1)
        self.send((data,), 0, 1)
        self.send((data,), 1, 0)
        pack(2)
        streams = (data,)
        if extra is not None:
            prepare()
            self.keep((extra,))
            self.send((extra,), 0, 1)
            self.send((extra,), 1, 0)
            streams = (extra, data)

        def more(g, c):
            pack(g + 1)
            self.send(streams, g, 0)
            return c

        lax.fori_loop(2, GROUPS - 1, more, 0)
        self.send(streams, GROUPS - 1, 0)

    def arrived(self, streams, g, count):
        for _, _, target, sent, got in streams:
            held = target.at[g, pl.ds(0, count)]
            pltpu.make_async_copy(held, held, sent.at[g]).wait()
            pltpu.make_async_copy(held, held, got.at[g]).wait()


def rank_rows(target_ref, key_ref, block):
    step = 256
    sub = lax.broadcasted_iota(I32, (DEVS, step), 0)
    lane = lax.broadcasted_iota(I32, (DEVS, step), 1)
    before = jnp.where(sub < lane, 1.0, 0.0).astype(BF)
    count = target_ref.shape[1]

    def ranks(b, seen):
        cols = pl.ds(pl.multiple_of(b * step, step), step)
        owner = lax.shift_right_logical(target_ref[:, cols], block.bit_length() - 1)
        mark = jnp.where(sub == owner, 1.0, 0.0)
        prior = mm(mark.astype(BF), before) + seen
        rank = jnp.sum(mark * prior, axis=0, keepdims=True).astype(I32)
        key_ref[:, cols] = owner * 16 + rank
        return seen + jnp.sum(mark, axis=1, keepdims=True)

    lax.fori_loop(0, count // step, ranks, jnp.zeros((DEVS, 1), F32))


def tag_rows(target_ref, key_ref, acc_ref, block, ranks):
    step = 256
    sub = lax.broadcasted_iota(I32, (DEVS, step), 0)
    nt = (((1,), (1,)), ((), ()))
    width = 256 * len(ranks)
    acc_ref[:, :width] = jnp.zeros((DEVS, width), F32)

    def some(b, c):
        cols = pl.ds(pl.multiple_of(b * step, step), step)
        key = key_ref[:, cols]
        rank = key & 15
        tag = (target_ref[:, cols] & (block - 1)) + 1
        high = lax.shift_right_logical(tag, 4).astype(F32)
        low = (tag & 15).astype(F32)
        marks = jnp.where(sub == lax.shift_right_logical(key, 4), 1.0, 0.0).astype(BF)
        picked = [
            jnp.where(rank == wanted, part, 0.0).astype(BF)
            for wanted in ranks
            for part in (high, low)
        ]
        picked = jnp.concatenate(picked, axis=0)
        acc_ref[:, :width] += lax.dot_general(marks, picked, nt, preferred_element_type=F32)
        return c

    lax.fori_loop(0, target_ref.shape[1] // step, some, 0)
    return [
        (acc_ref[:, i : i + 128] * 16.0 + acc_ref[:, i + 128 : i + 256]).astype(I32)
        for i in range(0, width, 256)
    ]


def packer(links, x_ref, key_ref, send_ref, full):
    width = x_ref.shape[1]
    half = width // 2
    tiles = send_ref.shape[2]
    column = lax.broadcasted_iota(I32, (256, 1), 0)
    slot = lax.shift_right_logical(column, 3)
    rank = column & 7
    first = lax.broadcasted_iota(I32, (SIDE, 8, half), 1) < 4

    def pack(g):
        plane = (links.plane + (slot & (PLANES - 1))) & (PLANES - 1)
        b = lax.shift_right_logical(slot, 3)
        spot = (links.spot + PLANES * b + ((g + 2 * b) & (PLANES - 1))) & (SIDE - 1)
        base = (plane * SIDE + spot) * 16

        def rows_of(wanted):
            picks = jnp.where(key_ref[...] == wanted, 1.0, 0.0).astype(BF)
            rows = mm(picks, x_ref[...])
            return rows[:, :half].reshape(SIDE, 8, half), rows[:, half:].reshape(SIDE, 8, half)

        if full:
            left, right = rows_of(base + rank)
            send_ref[g, :, 0] = left.astype(BF)
            send_ref[g, :, 1] = right.astype(BF)
        left, right = rows_of(base + full + (rank & 3))
        send_ref[g, :, tiles - 1] = jnp.where(first, left, right).astype(BF)

    return pack


def place_rows(got_ref, g, marks, out_ref, full):
    block, width = out_ref.shape
    half = width // 2
    tiles = got_ref.shape[2]
    chunk = min(block, 512)
    first = lax.broadcasted_iota(I32, (SIDE, 8, half), 1) < 4
    weights = []
    if full:
        left = got_ref[g, :, 0].astype(F32).reshape(256, half)
        right = got_ref[g, :, 1].astype(F32).reshape(256, half)
        weights.append(jnp.concatenate([left, right], axis=1).astype(BF))
    mixed = got_ref[g, :, tiles - 1].astype(F32)
    left = jnp.where(first, mixed, 0.0).reshape(256, half)
    right = jnp.where(first, 0.0, mixed).reshape(256, half)
    weights.append(jnp.concatenate([left, right], axis=1).astype(BF))
    weights = jnp.concatenate(weights, axis=0)
    rows = lax.broadcasted_iota(I32, (chunk, 1), 0) + 1

    def some(i, c):
        r0 = pl.multiple_of(i * chunk, chunk)
        picks = jnp.where(marks == rows + r0, 1.0, 0.0).astype(BF)
        at_rows = pl.ds(r0, chunk)
        out_ref[at_rows, :] = (out_ref[at_rows, :].astype(F32) + mm(picks, weights)).astype(BF)
        return c

    lax.fori_loop(0, block // chunk, some, 0)


def spread_kernel(
    full, inner, voxels, x_ref, target_ref, owner_ref, out_ref, key_out, marks_out,
    key_s, acc_s, send_s, tags_s, got_s, seen_s, d_send, d_recv, t_send, t_recv, ready,
):
    links = Links(inner)
    links.greet()
    block = out_ref.shape[0]
    rank_rows(target_ref, key_s, block)

    def prepare():
        rank_rows(owner_ref, key_out, voxels)
        eight = lax.broadcasted_iota(I32, (128, 1), 0) & 7
        four = eight & 3
        first, second = tag_rows(target_ref, key_s, acc_s, block, (eight, full + four))
        (third,) = tag_rows(owner_ref, key_out, acc_s, voxels, (four,))
        lane = lax.shift_right_logical(lax.broadcasted_iota(I32, (DEVS, 128), 1), 3)
        owner = lax.broadcasted_iota(I32, (DEVS, 1), 0)
        k = (lax.shift_right_logical(owner, 5) - links.plane) & (PLANES - 1)
        j = ((owner & (SIDE - 1)) - links.spot) & (SIDE - 1)
        slot = (lax.shift_right_logical(j, 3) & 1) * 8 + k
        tags = jnp.where(lane == slot, first + 4096 * second, 0)
        tags = jnp.where(lane == (slot + 8) & 15, third, tags)
        tags_s[...] = tags.reshape(PLANES, SIDE, 1, 128)
        out_ref[...] = jnp.zeros_like(out_ref)

    extra = (tags_s, True, seen_s, t_send, t_recv)
    data = (send_s, False, got_s, d_send, d_recv)
    links.send_all(data, packer(links, x_ref, key_s, send_s, full), ready, extra, prepare)
    streams = (extra, data)
    low = lax.broadcasted_iota(I32, (1, 128), 1) < 64

    def land(g, count):
        links.arrived(streams, g, count)
        points, later = [], []
        for part in range(2):
            a = jnp.sum(seen_s[g, part * 16 : part * 16 + 8], axis=0)
            b = jnp.sum(seen_s[g, part * 16 + 8 : part * 16 + 16], axis=0)
            points.append(jnp.where(low, a, b))
            other = jnp.where(low, b, a)
            later.append(jnp.concatenate([other[:, 64:], other[:, :64]], axis=1))
        points = jnp.concatenate(points, axis=1)
        marks_out[g] = jnp.concatenate(later, axis=1)
        marks = jnp.concatenate(
            [points & 4095, lax.shift_right_logical(points, 12)], axis=1
        )
        place_rows(got_s, g, marks, out_ref, full)

    land(0, SIDE - 1)

    def more(g, c):
        land(g, SIDE)
        return c

    lax.fori_loop(1, GROUPS, more, 0)


def spread(x, target, owner, capacity, inner):
    count, width = x.shape
    voxels = owner.shape[1]
    vm = pl.BlockSpec(memory_space=pltpu.VMEM)
    data = pltpu.VMEM((PLANES, SIDE, capacity // 4, 8, width // 2), BF)
    tags = pltpu.VMEM((PLANES, SIDE, 1, 128), I32)
    return pl.pallas_call(
        functools.partial(spread_kernel, capacity - 4, inner, voxels),
        out_shape=(
            jax.ShapeDtypeStruct((count, width), BF),
            jax.ShapeDtypeStruct((1, voxels), I32),
            jax.ShapeDtypeStruct((PLANES, 1, 256), I32),
        ),
        in_specs=[vm] * 3,
        out_specs=[vm] * 3,
        scratch_shapes=[
            pltpu.VMEM((1, count), I32), pltpu.VMEM((DEVS, 512), F32), data, tags, data, tags
        ]
        + [pltpu.SemaphoreType.DMA((PLANES,))] * 4
        + [pltpu.SemaphoreType.REGULAR],
        compiler_params=pltpu.CompilerParams(
            collective_id=1, has_side_effects=True, vmem_limit_bytes=56 * 2**20
        ),
        name="spread",
    )(x, target, owner)


def gather_kernel(
    inner, points_ref, att_ref, ids_ref, wout_ref, wup_ref, wdown_ref, key_ref, marks_ref, out_ref,
    fin_s, x_ref, send_s, got_s, d_send, d_recv, ready,
):
    links = Links(inner)
    links.greet()
    tail(points_ref, att_ref, ids_ref, wout_ref, wup_ref, wdown_ref, fin_s, x_ref)
    out_ref[...] = jnp.zeros_like(out_ref)
    data = (send_s, False, got_s, d_send, d_recv)
    links.send_all(data, packer(links, x_ref, key_ref, send_s, 0), ready)
    streams = (data,)

    def land(g, count):
        links.arrived(streams, g, count)
        place_rows(got_s, g, marks_ref[g], out_ref, 0)

    land(0, SIDE - 1)

    def more(g, c):
        land(g, SIDE)
        return c

    lax.fori_loop(1, GROUPS, more, 0)


def gather(points, att, ids, w_out, w_up, w_down, key, marks, inner):
    width = points.shape[1]
    count = key.shape[1]
    vm = pl.BlockSpec(memory_space=pltpu.VMEM)
    data = pltpu.VMEM((PLANES, SIDE, 1, 8, width // 2), BF)
    return pl.pallas_call(
        functools.partial(gather_kernel, inner),
        out_shape=jax.ShapeDtypeStruct((count, width), BF),
        in_specs=[vm] * 8,
        out_specs=vm,
        scratch_shapes=[pltpu.VMEM(points.shape, BF), pltpu.VMEM((count, width), BF), data, data]
        + [pltpu.SemaphoreType.DMA((PLANES,))] * 2
        + [pltpu.SemaphoreType.REGULAR],
        compiler_params=pltpu.CompilerParams(
            collective_id=2, has_side_effects=True, vmem_limit_bytes=56 * 2**20
        ),
        name="gather",
    )(points, att, ids, w_out, w_up, w_down, key, marks)


def finish_kernel(x_ref, w_ref, out_ref):
    block = 128

    def some(i, c):
        rows = pl.ds(pl.multiple_of(i * block, block), block)
        out_ref[rows, :] = gelu(normalize(mm(x_ref[rows, :], w_ref[...]))).astype(BF)
        return c

    lax.fori_loop(0, x_ref.shape[0] // block, some, 0)


def finish(x, w):
    vm = pl.BlockSpec(memory_space=pltpu.VMEM)
    return pl.pallas_call(
        finish_kernel,
        out_shape=jax.ShapeDtypeStruct((x.shape[0], w.shape[1]), BF),
        in_specs=[vm] * 2,
        out_specs=vm,
        name="finish",
    )(x, w)


def per_device(features, point_dest, cluster, owner_row, w_qkv, w_out, w_up, w_down, w_pool):
    inner = lax.axis_size("hd")
    points, key, marks = spread(
        features, point_dest.reshape(1, -1), owner_row.reshape(1, -1), 12, inner
    )
    att = attention(points, w_qkv)
    placed = gather(
        points, att, cluster.reshape(1, -1), w_out, w_up, w_down, key, marks, inner
    )
    return finish(placed, w_pool)


def solution(mesh):
    rows = P(("sp", "hd"), None)
    line = P(("sp", "hd"))
    return jax.shard_map(
        per_device,
        mesh=mesh,
        in_specs=(rows, line, line, line, P(), P(), P(), P(), P()),
        out_specs=rows,
        check_vma=False,
    )
```

```python
import functools
import jax
import jax.numpy as jnp
from jax import lax
from jax.experimental import pallas as pl
from jax.experimental.pallas import tpu as pltpu
from jax.sharding import PartitionSpec as P

BF = jnp.bfloat16
F32 = jnp.float32
I32 = jnp.int32
HS = 16
PATCH = 1024
EPSILON = 1e-05
LOG2E = 1.4426950408889634
SCALE = HS ** (-0.5) * LOG2E
SAFE = 100.0


def normalize(values):
    center = jnp.mean(values, axis=-1, keepdims=True)
    shifted = values - center
    spread = jnp.mean(shifted * shifted, axis=-1, keepdims=True)
    return shifted * lax.rsqrt(spread + EPSILON)


def gelu(values):
    return 0.5 * values * (1.0 + lax.erf(values * (0.5**0.5)))


def mm(a, b):
    return jnp.dot(a, b, preferred_element_type=F32)


def attention_kernel(
    points_ref, wqkv_ref, att_ref, wq_s, wv_s, k_s, q_s, v_s,
):
    rows_all, width = points_ref.shape
    heads = width // HS
    blk = 256
    groups = width // 128
    wq_s[...] = wqkv_ref[0].T
    wv_s[...] = wqkv_ref[2].T
    v_s[:, HS:, :] = jnp.ones((heads, HS, PATCH), BF)
    head_mask = (
        lax.broadcasted_iota(I32, (width, 128), 0) // HS
        == lax.broadcasted_iota(I32, (width, 128), 1)
    ).astype(BF)

    def patch(number, carry):
        base = number * PATCH

        def project(i, bound):
            qmax, kmax = bound
            r0 = pl.multiple_of(i * blk, blk)
            x = points_ref[pl.ds(pl.multiple_of(base + r0, blk), blk), :].astype(F32)
            normed = normalize(x).astype(BF)
            keys = mm(normed, wqkv_ref[1])
            for g in range(groups):
                k_s[g, pl.ds(r0, blk), :] = keys[:, g * 128 : (g + 1) * 128].astype(BF)
            nt = (((1,), (1,)), ((), ()))
            queries = lax.dot_general(wq_s[...], normed, nt, preferred_element_type=F32)
            values = lax.dot_general(wv_s[...], normed, nt, preferred_element_type=F32)
            q_s[:, pl.ds(r0, blk)] = queries.astype(BF)
            v_s[:, 0:HS, pl.ds(r0, blk)] = values.astype(BF).reshape(heads, HS, blk)
            knorm = mm((keys * keys).astype(BF), head_mask)
            qnorm = jnp.sum((queries * queries).reshape(heads, HS, blk), axis=1)
            return (jnp.maximum(qmax, qnorm), jnp.maximum(kmax, jnp.max(knorm, axis=0, keepdims=True)))

        qmax, kmax = lax.fori_loop(
            0, PATCH // blk, project,
            (jnp.zeros((heads, blk), F32), jnp.zeros((1, 128), F32)),
            unroll=2,
        )
        bound = 1.05 * SCALE * SCALE * jnp.max(qmax) * jnp.max(kmax)
        qb = 512
        sub = lax.broadcasted_iota(I32, (128, qb), 0) // HS

        def attend(shifted):
            def head(h, c):
                g = h // 8
                r0 = pl.multiple_of(h * HS, HS)
                for q0 in range(0, PATCH, qb):
                    q = q_s[pl.ds(r0, HS), q0 : q0 + qb]
                    q = jnp.concatenate([q] * 8, axis=0)
                    q = jnp.where(sub == h % 8, q, jnp.zeros_like(q))
                    scores = mm(k_s[g], q)
                    if shifted:
                        scores = scores - jnp.max(scores, axis=0, keepdims=True)
                    raised = jnp.exp2(scores * SCALE).astype(BF)
                    out = mm(v_s[h], raised)
                    att_ref[number, pl.ds(r0, HS), q0 : q0 + qb] = (out[:HS] / out[HS : HS + 1]).astype(BF)
                return c

            lax.fori_loop(0, heads, head, 0, unroll=1 if shifted else 4)

        @pl.when(bound <= SAFE * SAFE)
        def _():
            attend(False)

        @pl.when(jnp.logical_not(bound <= SAFE * SAFE))
        def _():
            attend(True)

        return carry

    lax.fori_loop(0, rows_all // PATCH, patch, 0)


def attention(points, w_qkv):
    rows, width = points.shape
    heads = width // HS
    vm = pl.BlockSpec(memory_space=pltpu.VMEM)
    return pl.pallas_call(
        attention_kernel,
        out_shape=jax.ShapeDtypeStruct((rows // PATCH, width, PATCH), BF),
        in_specs=[vm] * 2,
        out_specs=vm,
        scratch_shapes=[
            pltpu.VMEM((width, width), BF),
            pltpu.VMEM((width, width), BF),
            pltpu.VMEM((width // 128, PATCH, 128), BF),
            pltpu.VMEM((width, PATCH), BF),
            pltpu.VMEM((heads, 2 * HS, PATCH), BF),
        ],
        compiler_params=pltpu.CompilerParams(vmem_limit_bytes=56 * 2**20),
        name="attention",
    )(points, w_qkv)


def tail(points_ref, att_ref, ids_ref, wout_ref, wup_ref, wdown_ref, fin_s, means_ref, midway):
    rows_all = points_ref.shape[0]
    blk = 256
    per = PATCH // blk

    def mlp(i, c):
        rows = pl.ds(pl.multiple_of(i * blk, blk), blk)
        cols = pl.ds(pl.multiple_of(i % per * blk, blk), blk)
        attended = att_ref[i // per, :, cols].T
        middle = points_ref[rows, :].astype(F32) + mm(attended, wout_ref[...])
        normed = normalize(middle).astype(BF)
        hidden = gelu(mm(normed, wup_ref[...])).astype(BF)
        fin_s[rows, :] = (middle + mm(hidden, wdown_ref[...])).astype(BF)
        return c

    lax.fori_loop(0, rows_all // blk, mlp, 0, unroll=2)
    midway()
    ids = ids_ref[...] - jnp.min(ids_ref[...], axis=1, keepdims=True)
    vb = 128

    def pool(i, c):
        v0 = pl.multiple_of(i * vb, vb)
        marks = jnp.where(lax.broadcasted_iota(I32, (vb, rows_all), 0) + v0 == ids, 1.0, 0.0)
        tally = jnp.sum(marks, axis=1, keepdims=True)
        means_ref[pl.ds(v0, vb), :] = (mm(marks.astype(BF), fin_s[...]) / tally).astype(BF)
        return c

    lax.fori_loop(0, means_ref.shape[0] // vb, pool, 0, unroll=2)


PLANES = 8
SIDE = 32
DEVS = PLANES * SIDE
GROUPS = DEVS // SIDE
MESH = pl.DeviceIdType.MESH


class Links:
    def __init__(self, inner):
        self.inner = inner
        me = lax.axis_index("sp") * inner + lax.axis_index("hd")
        self.plane = lax.div(me, SIDE)
        self.spot = lax.rem(me, SIDE)

    def peer(self, k, j):
        return lax.rem(self.plane + k, PLANES), lax.rem(self.spot + j, SIDE)

    def device(self, plane, spot):
        number = plane * SIDE + spot
        return lax.div(number, self.inner), lax.rem(number, self.inner)

    def signal(self, sem, k, j):
        pl.semaphore_signal(
            sem, inc=1, device_id=self.device(*self.peer(k, j)), device_id_type=MESH
        )

    def greet(self):
        barrier = pltpu.get_barrier_semaphore()

        def up(k, c):
            self.signal(barrier, k, 0)
            return c

        def side(j, c):
            self.signal(barrier, 0, j)
            return c

        lax.fori_loop(1, PLANES, up, 0)
        lax.fori_loop(1, SIDE, side, 0)

    def pass_on(self, ready):
        pl.semaphore_wait(pltpu.get_barrier_semaphore(), PLANES - 1 + SIDE - 1)

        def up(k, c):
            self.signal(ready, k, 0)
            return c

        lax.fori_loop(1, PLANES, up, 0)

    def send(self, streams, g, start):
        def one(s, c):
            plane, spot = self.peer(
                lax.rem(s, PLANES), g * (SIDE // PLANES) + lax.div(s, PLANES)
            )
            for source, by_device, target, sent, got in streams:
                pltpu.make_async_remote_copy(
                    source.at[plane, spot] if by_device else source.at[g, s],
                    target.at[g, s], sent.at[g], got.at[g],
                    device_id=self.device(plane, spot), device_id_type=MESH,
                ).start()
            return c

        lax.fori_loop(start, SIDE, one, 0)

    def keep(self, streams):
        for source, by_device, target, _, _ in streams:
            target[0, 0] = source[self.plane, self.spot] if by_device else source[0, 0]

    def send_all(self, data, pack, ready, extra=None, prepare=None):
        pack(0)
        pack(1)
        self.keep((data,))
        pl.semaphore_wait(ready, PLANES - 1)
        self.send((data,), 0, 1)
        self.send((data,), 1, 0)
        pack(2)
        streams = (data,)
        if extra is not None:
            prepare()
            self.keep((extra,))
            self.send((extra,), 0, 1)
            self.send((extra,), 1, 0)
            streams = (extra, data)

        def more(g, c):
            pack(g + 1)
            self.send(streams, g, 0)
            return c

        lax.fori_loop(2, GROUPS - 1, more, 0)
        self.send(streams, GROUPS - 1, 0)

    def arrived(self, streams, g, count):
        for _, _, target, sent, got in streams:
            held = target.at[g, pl.ds(0, count)]
            pltpu.make_async_copy(held, held, sent.at[g]).wait()
            pltpu.make_async_copy(held, held, got.at[g]).wait()


def rank_rows(target_ref, key_ref, block):
    step = 256
    sub = lax.broadcasted_iota(I32, (DEVS, step), 0)
    lane = lax.broadcasted_iota(I32, (DEVS, step), 1)
    before = jnp.where(sub < lane, 1.0, 0.0).astype(BF)
    count = target_ref.shape[1]

    def ranks(b, seen):
        cols = pl.ds(pl.multiple_of(b * step, step), step)
        owner = lax.shift_right_logical(target_ref[:, cols], block.bit_length() - 1)
        mark = jnp.where(sub == owner, 1.0, 0.0)
        prior = mm(mark.astype(BF), before) + seen
        rank = jnp.sum(mark * prior, axis=0, keepdims=True).astype(I32)
        key_ref[:, cols] = owner * 16 + rank
        return seen + jnp.sum(mark, axis=1, keepdims=True)

    lax.fori_loop(0, count // step, ranks, jnp.zeros((DEVS, 1), F32), unroll=2)


def tag_rows(target_ref, key_ref, acc_ref, block, ranks):
    step = 256
    sub = lax.broadcasted_iota(I32, (DEVS, step), 0)
    nt = (((1,), (1,)), ((), ()))
    width = 256 * len(ranks)
    acc_ref[:, :width] = jnp.zeros((DEVS, width), F32)

    def some(b, c):
        cols = pl.ds(pl.multiple_of(b * step, step), step)
        key = key_ref[:, cols]
        rank = key & 15
        tag = (target_ref[:, cols] & (block - 1)) + 1
        high = lax.shift_right_logical(tag, 4).astype(F32)
        low = (tag & 15).astype(F32)
        marks = jnp.where(sub == lax.shift_right_logical(key, 4), 1.0, 0.0).astype(BF)
        picked = [
            jnp.where(rank == wanted, part, 0.0).astype(BF)
            for wanted in ranks
            for part in (high, low)
        ]
        picked = jnp.concatenate(picked, axis=0)
        acc_ref[:, :width] += lax.dot_general(marks, picked, nt, preferred_element_type=F32)
        return c

    lax.fori_loop(0, target_ref.shape[1] // step, some, 0)
    return [
        (acc_ref[:, i : i + 128] * 16.0 + acc_ref[:, i + 128 : i + 256]).astype(I32)
        for i in range(0, width, 256)
    ]


def packer(links, x_ref, key_ref, send_ref, full):
    width = x_ref.shape[1]
    half = width // 2
    tiles = send_ref.shape[2]
    column = lax.broadcasted_iota(I32, (256, 1), 0)
    slot = lax.shift_right_logical(column, 3)
    rank = column & 7
    first = lax.broadcasted_iota(I32, (SIDE, 8, half), 1) < 4

    def pack(g):
        plane = (links.plane + (slot & (PLANES - 1))) & (PLANES - 1)
        spot = (links.spot + g * (SIDE // PLANES) + lax.shift_right_logical(slot, 3)) & (SIDE - 1)
        base = (plane * SIDE + spot) * 16

        def rows_of(wanted):
            picks = jnp.where(key_ref[...] == wanted, 1.0, 0.0).astype(BF)
            rows = mm(picks, x_ref[...])
            return rows[:, :half].reshape(SIDE, 8, half), rows[:, half:].reshape(SIDE, 8, half)

        if full:
            left, right = rows_of(base + rank)
            send_ref[g, :, 0] = left.astype(BF)
            send_ref[g, :, 1] = right.astype(BF)
        left, right = rows_of(base + full + (rank & 3))
        send_ref[g, :, tiles - 1] = jnp.where(first, left, right).astype(BF)

    return pack


def place_rows(got_ref, g, marks, out_ref, full):
    block, width = out_ref.shape
    half = width // 2
    tiles = got_ref.shape[2]
    chunk = min(block, 512)
    first = lax.broadcasted_iota(I32, (SIDE, 8, half), 1) < 4
    weights = []
    if full:
        left = got_ref[g, :, 0].astype(F32).reshape(256, half)
        right = got_ref[g, :, 1].astype(F32).reshape(256, half)
        weights.append(jnp.concatenate([left, right], axis=1).astype(BF))
    mixed = got_ref[g, :, tiles - 1].astype(F32)
    left = jnp.where(first, mixed, 0.0).reshape(256, half)
    right = jnp.where(first, 0.0, mixed).reshape(256, half)
    weights.append(jnp.concatenate([left, right], axis=1).astype(BF))
    weights = jnp.concatenate(weights, axis=0)
    rows = lax.broadcasted_iota(I32, (chunk, 1), 0) + 1

    def some(i, c):
        r0 = pl.multiple_of(i * chunk, chunk)
        picks = jnp.where(marks == rows + r0, 1.0, 0.0).astype(BF)
        at_rows = pl.ds(r0, chunk)
        out_ref[at_rows, :] = (out_ref[at_rows, :].astype(F32) + mm(picks, weights)).astype(BF)
        return c

    lax.fori_loop(0, block // chunk, some, 0)


def spread_kernel(
    full, inner, voxels, x_ref, target_ref, owner_ref, out_ref, key_out, marks_out,
    key_s, acc_s, send_s, tags_s, got_s, seen_s, d_send, d_recv, t_send, t_recv, ready,
):
    links = Links(inner)
    links.greet()
    block = out_ref.shape[0]
    rank_rows(target_ref, key_s, block)
    links.pass_on(ready)

    def prepare():
        rank_rows(owner_ref, key_out, voxels)
        eight = lax.broadcasted_iota(I32, (128, 1), 0) & 7
        four = eight & 3
        first, second = tag_rows(target_ref, key_s, acc_s, block, (eight, full + four))
        (third,) = tag_rows(owner_ref, key_out, acc_s, voxels, (four,))
        lane = lax.shift_right_logical(lax.broadcasted_iota(I32, (DEVS, 128), 1), 3)
        owner = lax.broadcasted_iota(I32, (DEVS, 1), 0)
        k = (lax.shift_right_logical(owner, 5) - links.plane) & (PLANES - 1)
        j = ((owner & (SIDE - 1)) - links.spot) & (SIDE - 1)
        slot = (j & 1) * 8 + k
        tags = jnp.where(lane == slot, first + 4096 * second, 0)
        tags = jnp.where(lane == (slot + 8) & 15, third, tags)
        tags_s[...] = tags.reshape(PLANES, SIDE, 1, 128)
        out_ref[...] = jnp.zeros_like(out_ref)

    extra = (tags_s, True, seen_s, t_send, t_recv)
    data = (send_s, False, got_s, d_send, d_recv)
    links.send_all(data, packer(links, x_ref, key_s, send_s, full), ready, extra, prepare)
    streams = (extra, data)
    low = lax.broadcasted_iota(I32, (1, 128), 1) < 64

    def land(g, count):
        links.arrived(streams, g, count)
        points, later = [], []
        for part in range(2):
            a = jnp.sum(seen_s[g, part * 16 : part * 16 + 8], axis=0)
            b = jnp.sum(seen_s[g, part * 16 + 8 : part * 16 + 16], axis=0)
            points.append(jnp.where(low, a, b))
            other = jnp.where(low, b, a)
            later.append(jnp.concatenate([other[:, 64:], other[:, :64]], axis=1))
        points = jnp.concatenate(points, axis=1)
        marks_out[g] = jnp.concatenate(later, axis=1)
        marks = jnp.concatenate(
            [points & 4095, lax.shift_right_logical(points, 12)], axis=1
        )
        place_rows(got_s, g, marks, out_ref, full)

    land(0, SIDE - 1)

    def more(g, c):
        land(g, SIDE)
        return c

    lax.fori_loop(1, GROUPS, more, 0)


def spread(x, target, owner, capacity, inner):
    count, width = x.shape
    voxels = owner.shape[1]
    vm = pl.BlockSpec(memory_space=pltpu.VMEM)
    data = pltpu.VMEM((PLANES, SIDE, capacity // 4, 8, width // 2), BF)
    tags = pltpu.VMEM((PLANES, SIDE, 1, 128), I32)
    return pl.pallas_call(
        functools.partial(spread_kernel, capacity - 4, inner, voxels),
        out_shape=(
            jax.ShapeDtypeStruct((count, width), BF),
            jax.ShapeDtypeStruct((1, voxels), I32),
            jax.ShapeDtypeStruct((PLANES, 1, 256), I32),
        ),
        in_specs=[vm] * 3,
        out_specs=[vm] * 3,
        scratch_shapes=[
            pltpu.VMEM((1, count), I32), pltpu.VMEM((DEVS, 512), F32), data, tags, data, tags
        ]
        + [pltpu.SemaphoreType.DMA((PLANES,))] * 4
        + [pltpu.SemaphoreType.REGULAR],
        compiler_params=pltpu.CompilerParams(
            collective_id=1, has_side_effects=True, vmem_limit_bytes=56 * 2**20
        ),
        name="spread",
    )(x, target, owner)


def gather_kernel(
    inner, points_ref, att_ref, ids_ref, wout_ref, wup_ref, wdown_ref, key_ref, marks_ref, out_ref,
    fin_s, x_ref, send_s, got_s, d_send, d_recv, ready,
):
    links = Links(inner)
    links.greet()
    tail(
        points_ref, att_ref, ids_ref, wout_ref, wup_ref, wdown_ref, fin_s, x_ref,
        lambda: links.pass_on(ready),
    )
    out_ref[...] = jnp.zeros_like(out_ref)
    data = (send_s, False, got_s, d_send, d_recv)
    links.send_all(data, packer(links, x_ref, key_ref, send_s, 0), ready)
    streams = (data,)

    def land(g, count):
        links.arrived(streams, g, count)
        place_rows(got_s, g, marks_ref[g], out_ref, 0)

    land(0, SIDE - 1)

    def more(g, c):
        land(g, SIDE)
        return c

    lax.fori_loop(1, GROUPS, more, 0)


def gather(points, att, ids, w_out, w_up, w_down, key, marks, inner):
    width = points.shape[1]
    count = key.shape[1]
    vm = pl.BlockSpec(memory_space=pltpu.VMEM)
    data = pltpu.VMEM((PLANES, SIDE, 1, 8, width // 2), BF)
    return pl.pallas_call(
        functools.partial(gather_kernel, inner),
        out_shape=jax.ShapeDtypeStruct((count, width), BF),
        in_specs=[vm] * 8,
        out_specs=vm,
        scratch_shapes=[pltpu.VMEM(points.shape, BF), pltpu.VMEM((count, width), BF), data, data]
        + [pltpu.SemaphoreType.DMA((PLANES,))] * 2
        + [pltpu.SemaphoreType.REGULAR],
        compiler_params=pltpu.CompilerParams(
            collective_id=2, has_side_effects=True, vmem_limit_bytes=56 * 2**20
        ),
        name="gather",
    )(points, att, ids, w_out, w_up, w_down, key, marks)


def finish_kernel(x_ref, w_ref, out_ref):
    block = 128

    def some(i, c):
        rows = pl.ds(pl.multiple_of(i * block, block), block)
        out_ref[rows, :] = gelu(normalize(mm(x_ref[rows, :], w_ref[...]))).astype(BF)
        return c

    lax.fori_loop(0, x_ref.shape[0] // block, some, 0, unroll=2)


def finish(x, w):
    vm = pl.BlockSpec(memory_space=pltpu.VMEM)
    return pl.pallas_call(
        finish_kernel,
        out_shape=jax.ShapeDtypeStruct((x.shape[0], w.shape[1]), BF),
        in_specs=[vm] * 2,
        out_specs=vm,
        name="finish",
    )(x, w)


def per_device(features, point_dest, cluster, owner_row, w_qkv, w_out, w_up, w_down, w_pool):
    inner = lax.axis_size("hd")
    points, key, marks = spread(
        features, point_dest.reshape(1, -1), owner_row.reshape(1, -1), 12, inner
    )
    att = attention(points, w_qkv)
    placed = gather(
        points, att, cluster.reshape(1, -1), w_out, w_up, w_down, key, marks, inner
    )
    return finish(placed, w_pool)


def solution(mesh):
    rows = P(("sp", "hd"), None)
    line = P(("sp", "hd"))
    return jax.shard_map(
        per_device,
        mesh=mesh,
        in_specs=(rows, line, line, line, P(), P(), P(), P(), P()),
        out_specs=rows,
        check_vma=False,
    )
```

```python
import functools
import jax
import jax.numpy as jnp
from jax import lax
from jax.experimental import pallas as pl
from jax.experimental.pallas import tpu as pltpu
from jax.sharding import PartitionSpec as P

BF = jnp.bfloat16
F32 = jnp.float32
I32 = jnp.int32
HS = 16
PATCH = 1024
EPSILON = 1e-05
LOG2E = 1.4426950408889634
SCALE = HS ** (-0.5) * LOG2E
SAFE = 100.0


def normalize(values):
    center = jnp.mean(values, axis=-1, keepdims=True)
    shifted = values - center
    spread = jnp.mean(shifted * shifted, axis=-1, keepdims=True)
    return shifted * lax.rsqrt(spread + EPSILON)


def gelu(values):
    return 0.5 * values * (1.0 + lax.erf(values * (0.5**0.5)))


def mm(a, b):
    return jnp.dot(a, b, preferred_element_type=F32)


def attention_kernel(
    points_ref, wqkv_ref, att_ref, wq_s, wv_s, k_s, q_s, v_s,
):
    rows_all, width = points_ref.shape
    heads = width // HS
    blk = 256
    groups = width // 128
    wq_s[...] = wqkv_ref[0].T
    wv_s[...] = wqkv_ref[2].T
    v_s[:, HS:, :] = jnp.ones((heads, HS, PATCH), BF)
    head_mask = (
        lax.broadcasted_iota(I32, (width, 128), 0) // HS
        == lax.broadcasted_iota(I32, (width, 128), 1)
    ).astype(BF)

    def patch(number, carry):
        base = number * PATCH

        def project(i, bound):
            qmax, kmax = bound
            r0 = pl.multiple_of(i * blk, blk)
            x = points_ref[pl.ds(pl.multiple_of(base + r0, blk), blk), :].astype(F32)
            normed = normalize(x).astype(BF)
            keys = mm(normed, wqkv_ref[1])
            for g in range(groups):
                k_s[g, pl.ds(r0, blk), :] = keys[:, g * 128 : (g + 1) * 128].astype(BF)
            nt = (((1,), (1,)), ((), ()))
            queries = lax.dot_general(wq_s[...], normed, nt, preferred_element_type=F32)
            values = lax.dot_general(wv_s[...], normed, nt, preferred_element_type=F32)
            q_s[:, pl.ds(r0, blk)] = queries.astype(BF)
            v_s[:, 0:HS, pl.ds(r0, blk)] = values.astype(BF).reshape(heads, HS, blk)
            knorm = mm((keys * keys).astype(BF), head_mask)
            qnorm = jnp.sum((queries * queries).reshape(heads, HS, blk), axis=1)
            return (jnp.maximum(qmax, qnorm), jnp.maximum(kmax, jnp.max(knorm, axis=0, keepdims=True)))

        qmax, kmax = lax.fori_loop(
            0, PATCH // blk, project,
            (jnp.zeros((heads, blk), F32), jnp.zeros((1, 128), F32)),
            unroll=4,
        )
        bound = 1.05 * SCALE * SCALE * jnp.max(qmax) * jnp.max(kmax)
        qb = 512
        sub = lax.broadcasted_iota(I32, (128, qb), 0) // HS

        def attend(shifted):
            def head(h, c):
                g = h // 8
                r0 = pl.multiple_of(h * HS, HS)
                for q0 in range(0, PATCH, qb):
                    q = q_s[pl.ds(r0, HS), q0 : q0 + qb]
                    q = jnp.concatenate([q] * 8, axis=0)
                    q = jnp.where(sub == h % 8, q, jnp.zeros_like(q))
                    scores = mm(k_s[g], q)
                    if shifted:
                        scores = scores - jnp.max(scores, axis=0, keepdims=True)
                    raised = jnp.exp2(scores * SCALE).astype(BF)
                    out = mm(v_s[h], raised)
                    att_ref[number, pl.ds(r0, HS), q0 : q0 + qb] = (out[:HS] / out[HS : HS + 1]).astype(BF)
                return c

            lax.fori_loop(0, heads, head, 0, unroll=1 if shifted else 8)

        @pl.when(bound <= SAFE * SAFE)
        def _():
            attend(False)

        @pl.when(jnp.logical_not(bound <= SAFE * SAFE))
        def _():
            attend(True)

        return carry

    lax.fori_loop(0, rows_all // PATCH, patch, 0)


def attention(points, w_qkv):
    rows, width = points.shape
    heads = width // HS
    vm = pl.BlockSpec(memory_space=pltpu.VMEM)
    return pl.pallas_call(
        attention_kernel,
        out_shape=jax.ShapeDtypeStruct((rows // PATCH, width, PATCH), BF),
        in_specs=[vm] * 2,
        out_specs=vm,
        scratch_shapes=[
            pltpu.VMEM((width, width), BF),
            pltpu.VMEM((width, width), BF),
            pltpu.VMEM((width // 128, PATCH, 128), BF),
            pltpu.VMEM((width, PATCH), BF),
            pltpu.VMEM((heads, 2 * HS, PATCH), BF),
        ],
        compiler_params=pltpu.CompilerParams(vmem_limit_bytes=56 * 2**20),
        name="attention",
    )(points, w_qkv)


def tail(points_ref, att_ref, ids_ref, wout_ref, wup_ref, wdown_ref, fin_s, means_ref, midway):
    rows_all = points_ref.shape[0]
    blk = 256
    per = PATCH // blk

    def mlp(i, c):
        rows = pl.ds(pl.multiple_of(i * blk, blk), blk)
        cols = pl.ds(pl.multiple_of(i % per * blk, blk), blk)
        attended = att_ref[i // per, :, cols].T
        middle = points_ref[rows, :].astype(F32) + mm(attended, wout_ref[...])
        normed = normalize(middle).astype(BF)
        hidden = gelu(mm(normed, wup_ref[...])).astype(BF)
        fin_s[rows, :] = (middle + mm(hidden, wdown_ref[...])).astype(BF)
        return c

    lax.fori_loop(0, rows_all // blk, mlp, 0, unroll=4)
    midway()
    ids = ids_ref[...] - jnp.min(ids_ref[...], axis=1, keepdims=True)
    vb = 128

    def pool(i, c):
        v0 = pl.multiple_of(i * vb, vb)
        marks = jnp.where(lax.broadcasted_iota(I32, (vb, rows_all), 0) + v0 == ids, 1.0, 0.0)
        tally = jnp.sum(marks, axis=1, keepdims=True)
        means_ref[pl.ds(v0, vb), :] = (mm(marks.astype(BF), fin_s[...]) / tally).astype(BF)
        return c

    lax.fori_loop(0, means_ref.shape[0] // vb, pool, 0, unroll=4)


PLANES = 8
SIDE = 32
DEVS = PLANES * SIDE
GROUPS = DEVS // SIDE
MESH = pl.DeviceIdType.MESH


class Links:
    def __init__(self, inner):
        self.inner = inner
        me = lax.axis_index("sp") * inner + lax.axis_index("hd")
        self.plane = lax.div(me, SIDE)
        self.spot = lax.rem(me, SIDE)

    def peer(self, k, j):
        return lax.rem(self.plane + k, PLANES), lax.rem(self.spot + j, SIDE)

    def device(self, plane, spot):
        number = plane * SIDE + spot
        return lax.div(number, self.inner), lax.rem(number, self.inner)

    def signal(self, sem, k, j):
        pl.semaphore_signal(
            sem, inc=1, device_id=self.device(*self.peer(k, j)), device_id_type=MESH
        )

    def greet(self):
        barrier = pltpu.get_barrier_semaphore()

        def up(k, c):
            self.signal(barrier, k, 0)
            return c

        def side(j, c):
            self.signal(barrier, 0, j)
            return c

        lax.fori_loop(1, PLANES, up, 0)
        lax.fori_loop(1, SIDE, side, 0)

    def pass_on(self, ready):
        pl.semaphore_wait(pltpu.get_barrier_semaphore(), PLANES - 1 + SIDE - 1)

        def up(k, c):
            self.signal(ready, k, 0)
            return c

        lax.fori_loop(1, PLANES, up, 0)

    def send(self, streams, g, start):
        def one(s, c):
            plane, spot = self.peer(
                lax.rem(s, PLANES), g * (SIDE // PLANES) + lax.div(s, PLANES)
            )
            for source, by_device, target, sent, got in streams:
                pltpu.make_async_remote_copy(
                    source.at[plane, spot] if by_device else source.at[g, s],
                    target.at[g, s], sent.at[g], got.at[g],
                    device_id=self.device(plane, spot), device_id_type=MESH,
                ).start()
            return c

        lax.fori_loop(start, SIDE, one, 0)

    def keep(self, streams):
        for source, by_device, target, _, _ in streams:
            target[0, 0] = source[self.plane, self.spot] if by_device else source[0, 0]

    def send_all(self, data, pack, ready, extra=None, prepare=None):
        pack(0)
        pack(1)
        self.keep((data,))
        pl.semaphore_wait(ready, PLANES - 1)
        self.send((data,), 0, 1)
        self.send((data,), 1, 0)
        pack(2)
        streams = (data,)
        if extra is not None:
            prepare()
            self.keep((extra,))
            self.send((extra,), 0, 1)
            self.send((extra,), 1, 0)
            streams = (extra, data)

        def more(g, c):
            pack(g + 1)
            self.send(streams, g, 0)
            return c

        lax.fori_loop(2, GROUPS - 1, more, 0)
        self.send(streams, GROUPS - 1, 0)

    def arrived(self, streams, g, count):
        for _, _, target, sent, got in streams:
            held = target.at[g, pl.ds(0, count)]
            pltpu.make_async_copy(held, held, sent.at[g]).wait()
            pltpu.make_async_copy(held, held, got.at[g]).wait()


def rank_rows(target_ref, key_ref, block):
    step = 256
    sub = lax.broadcasted_iota(I32, (DEVS, step), 0)
    lane = lax.broadcasted_iota(I32, (DEVS, step), 1)
    before = jnp.where(sub < lane, 1.0, 0.0).astype(BF)
    count = target_ref.shape[1]

    def ranks(b, seen):
        cols = pl.ds(pl.multiple_of(b * step, step), step)
        owner = lax.shift_right_logical(target_ref[:, cols], block.bit_length() - 1)
        mark = jnp.where(sub == owner, 1.0, 0.0)
        prior = mm(mark.astype(BF), before) + seen
        rank = jnp.sum(mark * prior, axis=0, keepdims=True).astype(I32)
        key_ref[:, cols] = owner * 16 + rank
        return seen + jnp.sum(mark, axis=1, keepdims=True)

    lax.fori_loop(0, count // step, ranks, jnp.zeros((DEVS, 1), F32), unroll=2)


def tag_rows(target_ref, key_ref, acc_ref, block, ranks):
    step = 256
    sub = lax.broadcasted_iota(I32, (DEVS, step), 0)
    nt = (((1,), (1,)), ((), ()))
    width = 256 * len(ranks)
    acc_ref[:, :width] = jnp.zeros((DEVS, width), F32)

    def some(b, c):
        cols = pl.ds(pl.multiple_of(b * step, step), step)
        key = key_ref[:, cols]
        rank = key & 15
        tag = (target_ref[:, cols] & (block - 1)) + 1
        high = lax.shift_right_logical(tag, 4).astype(F32)
        low = (tag & 15).astype(F32)
        marks = jnp.where(sub == lax.shift_right_logical(key, 4), 1.0, 0.0).astype(BF)
        picked = [
            jnp.where(rank == wanted, part, 0.0).astype(BF)
            for wanted in ranks
            for part in (high, low)
        ]
        picked = jnp.concatenate(picked, axis=0)
        acc_ref[:, :width] += lax.dot_general(marks, picked, nt, preferred_element_type=F32)
        return c

    lax.fori_loop(0, target_ref.shape[1] // step, some, 0)
    return [
        (acc_ref[:, i : i + 128] * 16.0 + acc_ref[:, i + 128 : i + 256]).astype(I32)
        for i in range(0, width, 256)
    ]


def packer(links, x_ref, key_ref, send_ref, full):
    width = x_ref.shape[1]
    half = width // 2
    tiles = send_ref.shape[2]
    column = lax.broadcasted_iota(I32, (256, 1), 0)
    slot = lax.shift_right_logical(column, 3)
    rank = column & 7
    first = lax.broadcasted_iota(I32, (SIDE, 8, half), 1) < 4

    def pack(g):
        plane = (links.plane + (slot & (PLANES - 1))) & (PLANES - 1)
        spot = (links.spot + g * (SIDE // PLANES) + lax.shift_right_logical(slot, 3)) & (SIDE - 1)
        base = (plane * SIDE + spot) * 16

        def rows_of(wanted):
            picks = jnp.where(key_ref[...] == wanted, 1.0, 0.0).astype(BF)
            rows = mm(picks, x_ref[...])
            return rows[:, :half].reshape(SIDE, 8, half), rows[:, half:].reshape(SIDE, 8, half)

        if full:
            left, right = rows_of(base + rank)
            send_ref[g, :, 0] = left.astype(BF)
            send_ref[g, :, 1] = right.astype(BF)
        left, right = rows_of(base + full + (rank & 3))
        send_ref[g, :, tiles - 1] = jnp.where(first, left, right).astype(BF)

    return pack


def place_rows(got_ref, g, marks, out_ref, full):
    block, width = out_ref.shape
    half = width // 2
    tiles = got_ref.shape[2]
    chunk = min(block, 512)
    first = lax.broadcasted_iota(I32, (SIDE, 8, half), 1) < 4
    weights = []
    if full:
        left = got_ref[g, :, 0].astype(F32).reshape(256, half)
        right = got_ref[g, :, 1].astype(F32).reshape(256, half)
        weights.append(jnp.concatenate([left, right], axis=1).astype(BF))
    mixed = got_ref[g, :, tiles - 1].astype(F32)
    left = jnp.where(first, mixed, 0.0).reshape(256, half)
    right = jnp.where(first, 0.0, mixed).reshape(256, half)
    weights.append(jnp.concatenate([left, right], axis=1).astype(BF))
    weights = jnp.concatenate(weights, axis=0)
    rows = lax.broadcasted_iota(I32, (chunk, 1), 0) + 1

    def some(i, c):
        r0 = pl.multiple_of(i * chunk, chunk)
        picks = jnp.where(marks == rows + r0, 1.0, 0.0).astype(BF)
        at_rows = pl.ds(r0, chunk)
        out_ref[at_rows, :] = (out_ref[at_rows, :].astype(F32) + mm(picks, weights)).astype(BF)
        return c

    lax.fori_loop(0, block // chunk, some, 0)


def spread_kernel(
    full, inner, voxels, x_ref, target_ref, owner_ref, out_ref, key_out, marks_out,
    key_s, acc_s, send_s, tags_s, got_s, seen_s, d_send, d_recv, t_send, t_recv, ready,
):
    links = Links(inner)
    links.greet()
    block = out_ref.shape[0]
    rank_rows(target_ref, key_s, block)
    links.pass_on(ready)

    def prepare():
        rank_rows(owner_ref, key_out, voxels)
        eight = lax.broadcasted_iota(I32, (128, 1), 0) & 7
        four = eight & 3
        first, second = tag_rows(target_ref, key_s, acc_s, block, (eight, full + four))
        (third,) = tag_rows(owner_ref, key_out, acc_s, voxels, (four,))
        lane = lax.shift_right_logical(lax.broadcasted_iota(I32, (DEVS, 128), 1), 3)
        owner = lax.broadcasted_iota(I32, (DEVS, 1), 0)
        k = (lax.shift_right_logical(owner, 5) - links.plane) & (PLANES - 1)
        j = ((owner & (SIDE - 1)) - links.spot) & (SIDE - 1)
        slot = (j & 1) * 8 + k
        tags = jnp.where(lane == slot, first + 4096 * second, 0)
        tags = jnp.where(lane == (slot + 8) & 15, third, tags)
        tags_s[...] = tags.reshape(PLANES, SIDE, 1, 128)
        out_ref[...] = jnp.zeros_like(out_ref)

    extra = (tags_s, True, seen_s, t_send, t_recv)
    data = (send_s, False, got_s, d_send, d_recv)
    links.send_all(data, packer(links, x_ref, key_s, send_s, full), ready, extra, prepare)
    streams = (extra, data)
    low = lax.broadcasted_iota(I32, (1, 128), 1) < 64

    def land(g, count):
        links.arrived(streams, g, count)
        points, later = [], []
        for part in range(2):
            a = jnp.sum(seen_s[g, part * 16 : part * 16 + 8], axis=0)
            b = jnp.sum(seen_s[g, part * 16 + 8 : part * 16 + 16], axis=0)
            points.append(jnp.where(low, a, b))
            other = jnp.where(low, b, a)
            later.append(jnp.concatenate([other[:, 64:], other[:, :64]], axis=1))
        points = jnp.concatenate(points, axis=1)
        marks_out[g] = jnp.concatenate(later, axis=1)
        marks = jnp.concatenate(
            [points & 4095, lax.shift_right_logical(points, 12)], axis=1
        )
        place_rows(got_s, g, marks, out_ref, full)

    land(0, SIDE - 1)

    def more(g, c):
        land(g, SIDE)
        return c

    lax.fori_loop(1, GROUPS, more, 0)


def spread(x, target, owner, capacity, inner):
    count, width = x.shape
    voxels = owner.shape[1]
    vm = pl.BlockSpec(memory_space=pltpu.VMEM)
    data = pltpu.VMEM((PLANES, SIDE, capacity // 4, 8, width // 2), BF)
    tags = pltpu.VMEM((PLANES, SIDE, 1, 128), I32)
    return pl.pallas_call(
        functools.partial(spread_kernel, capacity - 4, inner, voxels),
        out_shape=(
            jax.ShapeDtypeStruct((count, width), BF),
            jax.ShapeDtypeStruct((1, voxels), I32),
            jax.ShapeDtypeStruct((PLANES, 1, 256), I32),
        ),
        in_specs=[vm] * 3,
        out_specs=[vm] * 3,
        scratch_shapes=[
            pltpu.VMEM((1, count), I32), pltpu.VMEM((DEVS, 512), F32), data, tags, data, tags
        ]
        + [pltpu.SemaphoreType.DMA((PLANES,))] * 4
        + [pltpu.SemaphoreType.REGULAR],
        compiler_params=pltpu.CompilerParams(
            collective_id=1, has_side_effects=True, vmem_limit_bytes=56 * 2**20
        ),
        name="spread",
    )(x, target, owner)


def gather_kernel(
    inner, points_ref, att_ref, ids_ref, wout_ref, wup_ref, wdown_ref, key_ref, marks_ref, out_ref,
    fin_s, x_ref, send_s, got_s, d_send, d_recv, ready,
):
    links = Links(inner)
    links.greet()
    tail(
        points_ref, att_ref, ids_ref, wout_ref, wup_ref, wdown_ref, fin_s, x_ref,
        lambda: links.pass_on(ready),
    )
    out_ref[...] = jnp.zeros_like(out_ref)
    data = (send_s, False, got_s, d_send, d_recv)
    links.send_all(data, packer(links, x_ref, key_ref, send_s, 0), ready)
    streams = (data,)

    def land(g, count):
        links.arrived(streams, g, count)
        place_rows(got_s, g, marks_ref[g], out_ref, 0)

    land(0, SIDE - 1)

    def more(g, c):
        land(g, SIDE)
        return c

    lax.fori_loop(1, GROUPS, more, 0)


def gather(points, att, ids, w_out, w_up, w_down, key, marks, inner):
    width = points.shape[1]
    count = key.shape[1]
    vm = pl.BlockSpec(memory_space=pltpu.VMEM)
    data = pltpu.VMEM((PLANES, SIDE, 1, 8, width // 2), BF)
    return pl.pallas_call(
        functools.partial(gather_kernel, inner),
        out_shape=jax.ShapeDtypeStruct((count, width), BF),
        in_specs=[vm] * 8,
        out_specs=vm,
        scratch_shapes=[pltpu.VMEM(points.shape, BF), pltpu.VMEM((count, width), BF), data, data]
        + [pltpu.SemaphoreType.DMA((PLANES,))] * 2
        + [pltpu.SemaphoreType.REGULAR],
        compiler_params=pltpu.CompilerParams(
            collective_id=2, has_side_effects=True, vmem_limit_bytes=56 * 2**20
        ),
        name="gather",
    )(points, att, ids, w_out, w_up, w_down, key, marks)


def finish_kernel(x_ref, w_ref, out_ref):
    block = 128

    def some(i, c):
        rows = pl.ds(pl.multiple_of(i * block, block), block)
        out_ref[rows, :] = gelu(normalize(mm(x_ref[rows, :], w_ref[...]))).astype(BF)
        return c

    lax.fori_loop(0, x_ref.shape[0] // block, some, 0, unroll=4)


def finish(x, w):
    vm = pl.BlockSpec(memory_space=pltpu.VMEM)
    return pl.pallas_call(
        finish_kernel,
        out_shape=jax.ShapeDtypeStruct((x.shape[0], w.shape[1]), BF),
        in_specs=[vm] * 2,
        out_specs=vm,
        name="finish",
    )(x, w)


def per_device(features, point_dest, cluster, owner_row, w_qkv, w_out, w_up, w_down, w_pool):
    inner = lax.axis_size("hd")
    points, key, marks = spread(
        features, point_dest.reshape(1, -1), owner_row.reshape(1, -1), 12, inner
    )
    att = attention(points, w_qkv)
    placed = gather(
        points, att, cluster.reshape(1, -1), w_out, w_up, w_down, key, marks, inner
    )
    return finish(placed, w_pool)


def solution(mesh):
    rows = P(("sp", "hd"), None)
    line = P(("sp", "hd"))
    return jax.shard_map(
        per_device,
        mesh=mesh,
        in_specs=(rows, line, line, line, P(), P(), P(), P(), P()),
        out_specs=rows,
        check_vma=False,
    )
```
